32 devices in a mesh: parts: 2 (over y), seq: 4 (over z), grp: 2 (over x), sub: 2 (over core).
Axes of the slice: x: 2, y: 2, z: 4, core: 2. Of those that a mesh axis runs over, the one named last changes fastest.
Arguments:
- projected: bfloat16 [2048, 3, 4096], P(('parts', 'seq'), None, ('grp', 'sub')), parts along dimension 0, may hold values from -6 to 6
- short_filter: float32 [3, 3, 4096], P(None, None, ('grp', 'sub')), may hold values from -3.5 to 3.5
- span_lengths: int32 [16], P('parts'), parts along dimension 0, may hold values from 1 to 512, 1024 in all
- mode_rates: float32 [8, 256], P(None, ('grp', 'sub')), may hold values from 4.8828126e-05 to 0.05
- mode_residues: float32 [8, 256], P(None, ('grp', 'sub')), may hold values from -2 to 2
- out_weight: bfloat16 [4096, 4096], P(None, ('grp', 'sub')), may hold values from -0.09375 to 0.09375
Outputs:
- mixed: bfloat16 [2048, 4096], P(('parts', 'seq'), ('grp', 'sub')), parts along dimension 0
The draws below stay inside these ranges and needn't reach their ends.
There are 2 independent parts, one for each index of `parts`. The reference program is written for one: setup_inputs(seed, part) draws one part's arguments, and reference() takes and returns one part's arrays. A program takes and returns all parts, laid end to end along the dimension named above; an argument that names none is the same for every part. Nothing has to cross between parts.
Inputs may be any that keep to these rules, and one draw needn't show every extreme that they name: `span_lengths`: the 8 span lengths, in order, sum to 1024; the longest has exactly 512 tokens.
All inputs are finite; a program needn't handle non-finite values.
Results may differ from the reference program's by a relative error of at most 0.0058.
Values may be sent and summed in bfloat16 or wider, within the bound.
A program may use at most 64 MiB of HBM per device.

```python
import math
import jax
import jax.numpy as jnp
import numpy as np
from jax import lax

D = 4096
SHORT = 3
FG = 256
NMODE = 8
NCHUNK = 8
LENGTH = 1024


def steps_of(own_key, dims, split, least, high):
    factor_of = 1.0
    for position, shards_of in split:
        draws = jax.random.uniform(jax.random.fold_in(jax.random.fold_in(own_key, 6), position), (shards_of,), jnp.float32, least / len(split), high / len(split))
        factor_of = factor_of * jnp.repeat(jnp.exp(draws), dims[position] // shards_of).reshape((-1,) + (1,) * (len(dims) - 1 - position))
    return factor_of


def split_up(number_of, total, reach, lean):
    loads = [(1 << 20) // math.isqrt(grade ** lean) + 1 for grade in range(2, number_of + 1)]
    surplus, counts = total - reach - (number_of - 1), [1] * (number_of - 1)
    while surplus > 0:
        candidates = [i for i in range(number_of - 1) if counts[i] < reach]
        pool, budget = sum([loads[i] for i in candidates]), surplus
        for i in candidates:
            addition = min(reach - counts[i], max(1, budget * loads[i] // pool), surplus)
            counts[i] = counts[i] + addition
            surplus = surplus - addition
    return np.array([reach] + counts)


def ragged_sizes(rng, number_of, total, limit, lean):
    if number_of == 2:
        one = jax.random.randint(rng, (), max(1, total - limit), min(limit, total - 1) + 1)
        return jnp.stack([one, total - one])
    tallies = jnp.asarray(split_up(number_of, total, limit, lean), jnp.int32)
    twos = (number_of - 1) // 2
    giver, sink = tallies[1:1 + 2 * twos:2], tallies[2:2 + 2 * twos:2]
    slack = jnp.minimum(giver - 1, limit - sink)
    moved = jax.random.randint(jax.random.fold_in(rng, 1), (twos,), 0, 1 << 20) % (slack + 1)
    tallies = tallies.at[1:1 + 2 * twos:2].set(giver - moved).at[2:2 + 2 * twos:2].set(sink + moved)
    return tallies[jax.random.permutation(jax.random.fold_in(rng, 2), number_of)]


def bell_draw(rng, extent, width, reach, split=(), held_as=jnp.bfloat16):
    drawn = jax.random.normal(rng, extent, jnp.float32) * width
    if len(split) > 0:
        drawn = steps_of(rng, extent, split, -0.22, 0.18) * drawn
    return jnp.clip(drawn, min=-reach, max=reach).astype(held_as)


def setup_inputs(seed: int = 0, part: int = 0) -> dict:
    key_list = jax.random.split(jax.random.key(seed), 7)
    own_keys = jax.random.split(jax.random.fold_in(key_list[6], part), 7)
    projected = bell_draw(own_keys[0], (LENGTH, 3, D), 1.0, 6.0, ((0, 4), (2, 4)))
    short_filter = bell_draw(key_list[1], (SHORT, 3, D), 3 ** -0.5, 3.5, ((2, 4),), jnp.float32)
    span_lengths = ragged_sizes(own_keys[2], NCHUNK, LENGTH, LENGTH // 2, 2).astype(jnp.int32)
    mode_rates = jnp.clip(jnp.exp(math.log(0.05) - 6.931472 * jax.random.uniform(key_list[3], (NMODE, FG), jnp.float32) ** steps_of(key_list[3], (NMODE, FG), ((1, 4),), -0.2, 0.2)), 4.882812572759576e-05, 0.05)
    mode_residues = bell_draw(key_list[4], (NMODE, FG), 0.35, 2.0, ((1, 4),), jnp.float32)
    out_weight = bell_draw(key_list[5], (D, D), D ** -0.5, 0.09375, ((1, 4),))
    return dict(projected=projected, short_filter=short_filter, span_lengths=span_lengths, mode_rates=mode_rates, mode_residues=mode_residues, out_weight=out_weight)


def span_index(span_lengths, positions):
    span_starts = (jnp.cumsum(span_lengths) - span_lengths).astype(jnp.int32)
    inside = (positions[:, None] >= span_starts[None, :]).astype(jnp.int32)
    return (lax.optimization_barrier(jnp.sum(inside, axis=1)) - 1).astype(jnp.int32)

def reference(projected, short_filter, span_lengths, mode_rates, mode_residues, out_weight):
    positions = jnp.arange(LENGTH, dtype=jnp.int32)
    span_of = span_index(span_lengths, positions)
    source = projected.astype(jnp.float32)
    filtered = short_filter[0][None] * source
    for tap_index in range(1, SHORT):
        shifted = jnp.concatenate([jnp.zeros((tap_index, 3, D), jnp.float32), source[:-tap_index]], axis=0)
        earlier = span_index(span_lengths, (positions - tap_index).astype(jnp.int32))
        same_span = (earlier == span_of).astype(jnp.float32)
        filtered = filtered + short_filter[tap_index][None] * shifted * same_span[:, None, None]
    gated_rows = (filtered[:, 1] * filtered[:, 2]).astype(jnp.bfloat16)
    group_size = D // FG
    decay_mode = jnp.repeat(jnp.exp(-mode_rates), group_size, axis=1)
    mode_weight = jnp.repeat(mode_residues * jnp.sqrt(-jnp.expm1(-2.0 * mode_rates)), group_size, axis=1)
    keep_flag = (span_of == span_index(span_lengths, (positions - 1).astype(jnp.int32))).astype(jnp.float32)

    def advance(carried, inputs):
        gated_row, keep_row = inputs
        carried = decay_mode * carried * keep_row + gated_row[None, :]
        return (carried, lax.optimization_barrier(jnp.sum(mode_weight * carried, axis=0)))
    _, long_out = lax.scan(advance, jnp.zeros((NMODE, D), jnp.float32), (gated_rows.astype(jnp.float32), keep_flag))
    mixed_in = (filtered[:, 0] * long_out).astype(jnp.bfloat16)
    return jnp.dot(mixed_in, out_weight, preferred_element_type=jnp.float32).astype(jnp.bfloat16)
```

```python
import functools

import jax
import jax.numpy as jnp
from jax import lax
from jax.experimental import pallas as pl
from jax.experimental.pallas import tpu as pltpu
from jax.sharding import PartitionSpec as P

MESH = pl.DeviceIdType.MESH
LANES = 128
HEAD = 8
EDGE = 16
F32, BF16 = jnp.float32, jnp.bfloat16


def tanh(x):
    x = jnp.clip(x, -7.90531110763549805, 7.90531110763549805)
    square = x * x
    top = jnp.full_like(x, -2.76076847742355e-16)
    for c in (
        2.00018790482477e-13, -8.60467152213735e-11, 5.12229709037114e-08,
        1.48572235717979e-05, 6.37261928875436e-04, 4.89352455891786e-03,
    ):
        top = top * square + c
    bottom = jnp.full_like(x, 1.19825839466702e-06)
    for c in (1.18534705686654e-04, 2.26843463243900e-03, 4.89352518554385e-03):
        bottom = bottom * square + c
    return jnp.where(jnp.abs(x) < 0.0004, x, x * top / bottom)


def kernel(
    sizes, spans_hbm, x_hbm, taps_hbm, rates_hbm, residues_hbm, weight_hbm, out_ref,
    spans_ref, x_ref, edge_ref, taps_ref, rates_ref, residues_ref, weight,
    wide_q, wide_k, wide_v, keep1, keep2, powers, mode_rows, wide_rates,
    gates, rows_out, mix_rows, halo_rows, halo_out, halo_in, state_out, state_in, incoming,
    gathered, total,
    load_sems, weight_sem, halo_send, halo_recv, state_send, state_recv,
    sub_send, sub_recv, grp_send, grp_recv, fwd_send, fwd_recv,
):
    seq, grp, sub, reach_steps, pieces, groupings = sizes
    _, tokens, channels = x_ref.shape
    modes, groups = rates_ref.shape
    rows = channels // LANES
    pitch = gates.shape[0] // tokens
    group_size = channels // groups
    per_row = LANES // group_size
    steps = range(1, reach_steps + 1)
    z, g, s = lax.axis_index("seq"), lax.axis_index("grp"), lax.axis_index("sub")
    offset = z * tokens

    loads = [
        pltpu.make_async_copy(source, target, load_sems.at[i])
        for i, (source, target) in enumerate((
            (rates_hbm, rates_ref), (residues_hbm, residues_ref), (spans_hbm, spans_ref),
            (x_hbm.at[:, pl.ds(tokens - EDGE, EDGE), :], edge_ref), (taps_hbm, taps_ref),
            (x_hbm.at[pl.ds(1, 2)], x_ref.at[pl.ds(1, 2)]), (x_hbm.at[pl.ds(0, 1)], x_ref.at[pl.ds(0, 1)]),
        ))
    ]
    load_rates, load_residues, load_spans, load_edge, load_taps, load_kv, load_q = loads
    for load in loads:
        load.start()

    barrier = pltpu.get_barrier_semaphore()
    for step in steps:
        @pl.when(z >= step)
        def _():
            pl.semaphore_signal(barrier, inc=1, device_id={"seq": z - step}, device_id_type=MESH)
    for axis, me, count in (("grp", g, grp), ("sub", s, sub)):
        for step in range(1, count):
            pl.semaphore_signal(
                barrier, inc=1, device_id={axis: lax.rem(me + step, count)}, device_id_type=MESH
            )
    load_weight = pltpu.make_async_copy(weight_hbm, weight, weight_sem)
    load_weight.start()

    if pitch != rows:
        for buffer in (gates, mode_rows):
            buffer[...] = jnp.zeros_like(buffer)
    incoming[...] = jnp.zeros_like(incoming)

    load_spans.wait()
    starts, start = [], jnp.int32(0)
    for i in range(spans_ref.shape[0]):
        starts.append(start)
        start = start + spans_ref[i]
    latest = jnp.int32(0)
    for first in starts:
        latest = jnp.where(first < offset + tokens, first, latest)
    position = offset - HEAD + lax.broadcasted_iota(jnp.int32, (tokens + HEAD, LANES), 0)
    here = position == starts[0]
    for first in starts[1:]:
        here = here | (position == first)
    keep1[...] = jnp.where(here, 0.0, 1.0)
    keep2[...] = keep1[pl.ds(HEAD, tokens), :] * keep1[pl.ds(HEAD - 1, tokens), :]

    load_rates.wait()
    load_residues.wait()
    rates = rates_ref[...]
    token = lax.broadcasted_iota(jnp.int32, (modes, tokens), 1)
    ahead = (token - (tokens - 1)).astype(F32)
    live = jnp.where(offset + token >= latest, 1.0, 0.0)
    for c in range(rows):
        for i in range(per_row):
            rate = jnp.broadcast_to(rates[:, c * per_row + i : c * per_row + i + 1], (modes, tokens))
            power = jnp.exp(rate * ahead) * live
            high = power.astype(BF16).astype(F32)
            wide_at = pl.ds(i * modes, modes)
            powers[c, wide_at, :] = high
            powers[c, pl.ds((per_row + i) * modes, modes), :] = power - high

    spread = (
        lax.broadcasted_iota(jnp.int32, (groups, channels), 1) // group_size
        == lax.broadcasted_iota(jnp.int32, (groups, channels), 0)
    ).astype(F32)
    drop = tanh(rates) * (1.0 + jnp.exp(-2.0 * rates))
    for first, values in ((0, rates), (modes, residues_ref[...] * jnp.sqrt(drop))):
        wide = jnp.dot(values, spread, precision=lax.Precision.HIGHEST, preferred_element_type=F32)
        if first == 0:
            wide_rates[...] = wide
        for c in range(rows):
            mode_rows[pl.ds(first * pitch + c, modes, stride=pitch), :] = wide[
                :, c * LANES : (c + 1) * LANES
            ]

    load_edge.wait()
    for j in range(3):
        for c in range(rows):
            lanes = slice(c * LANES, (c + 1) * LANES)
            halo_rows[pl.ds(2 * j * pitch + c, 2, stride=pitch), :] = edge_ref[j, :, lanes].astype(F32)[EDGE - 2 :]
    halo_out[...] = halo_rows[...].astype(BF16)

    pl.semaphore_wait(barrier, jnp.minimum(reach_steps, seq - 1 - z) + grp + sub - 2)

    send_halo = pltpu.make_async_remote_copy(
        src_ref=halo_out, dst_ref=halo_in, send_sem=halo_send, recv_sem=halo_recv,
        device_id={"seq": lax.rem(z + 1, seq)}, device_id_type=MESH,
    )

    @pl.when(z < seq - 1)
    def _():
        send_halo.start()

    load_taps.wait()

    def lanes_of(c):
        return pl.ds(pl.multiple_of(c * LANES, LANES), LANES)

    def filtered(j, buffer, c, lower, count):
        tap = [taps_ref[k, pl.ds(j, 1), lanes_of(c)] for k in range(3)]
        now, last, older = (buffer[c, pl.ds(HEAD + lower - k, count), :] for k in range(3))
        m1, m2 = keep1[pl.ds(HEAD + lower, count), :], keep2[pl.ds(lower, count), :]
        return tap[0] * now + tap[1] * last * m1 + tap[2] * older * m2

    def gate(c, lower, count):
        value = (filtered(1, wide_k, c, lower, count) * filtered(2, wide_v, c, lower, count)).astype(BF16)
        gathered[0, pl.ds(lower, count), lanes_of(c)] = value
        gates[pl.ds(lower * pitch + c, count, stride=pitch), :] = value.astype(F32)

    load_kv.wait()
    block = 48

    def gate_rows(c, carry):
        for j, buffer in ((1, wide_k), (2, wide_v)):
            buffer[c, pl.ds(HEAD, tokens), :] = x_ref[j, :, lanes_of(c)].astype(F32)
        lower = EDGE
        while lower < tokens:
            count = min(block, tokens - lower)
            gate(c, lower, count)
            lower += count
        return carry

    lax.fori_loop(0, rows, gate_rows, 0)

    @pl.when(z == 0)
    def _():
        halo_in[...] = jnp.zeros_like(halo_in)

    @pl.when(z > 0)
    def _():
        send_halo.wait_recv()

    halo_rows[...] = halo_in[...].astype(F32)
    for j, buffer in enumerate((wide_q, wide_k, wide_v)):
        for c in range(rows):
            buffer[c, pl.ds(HEAD - 2, 2), :] = halo_rows[pl.ds(2 * j * pitch + c, 2, stride=pitch), :]

    lane_group = lax.broadcasted_iota(jnp.int32, (modes, LANES), 1) // group_size

    def end_state(c, carry):
        gate(c, 0, EDGE)
        sums = jnp.dot(powers[c].astype(BF16), gathered[0, :, lanes_of(c)], preferred_element_type=F32)
        sums = sums[: per_row * modes] + sums[per_row * modes :]
        state = sums[:modes]
        for i in range(1, per_row):
            state = jnp.where(lane_group == i, sums[i * modes : (i + 1) * modes], state)
        state_out[:, lanes_of(c)] = state
        return carry

    lax.fori_loop(0, rows, end_state, 0)

    state_copies = []
    for step in steps:
        copy = pltpu.make_async_remote_copy(
            src_ref=state_out, dst_ref=state_in.at[step - 1],
            send_sem=state_send.at[step - 1], recv_sem=state_recv.at[step - 1],
            device_id={"seq": lax.rem(z + step, seq)}, device_id_type=MESH,
        )
        state_copies.append(copy)
    for step in reversed(steps):
        pl.when(z + step < seq)(state_copies[step - 1].start)

    def tile(ref, index):
        return ref[pl.ds(pl.multiple_of(index * pitch, pitch), pitch), :]

    decay = [jnp.exp(-tile(mode_rows, n)) for n in range(modes)]
    gain = [tile(mode_rows, modes + n) for n in range(modes)]
    load_q.wait()

    def widen_q(c, carry):
        wide_q[c, pl.ds(HEAD, tokens), :] = x_ref[0, :, lanes_of(c)].astype(F32)
        return carry

    lax.fori_loop(0, rows, widen_q, 0)

    for step in steps:
        reach = (step - 1) * tokens
        open_ = jnp.float32(1.0)
        for first in starts:
            inside = (first >= offset - reach) & (first <= offset - 1)
            open_ = jnp.where(inside, 0.0, open_)

        @pl.when(z >= step)
        def _():
            state_copies[step - 1].wait_recv()
            for c in range(rows):
                lanes = slice(c * LANES, (c + 1) * LANES)
                part = state_in[step - 1, :, lanes] * open_
                if reach:
                    part = part * jnp.exp(wide_rates[:, lanes] * (-float(reach)))
                at = pl.ds(c, modes, stride=pitch)
                incoming[at, :] = incoming[at, :] + part

    own = g * sub + s
    carried = [tile(incoming, n) for n in range(modes)]
    unroll = 8

    def combine(parts):
        while len(parts) > 1:
            parts = [sum(parts[i + 1 : i + 2], parts[i]) for i in range(0, len(parts), 2)]
        return parts[0]

    def advance(block, state):
        for u in range(unroll):
            t = block * unroll + u
            gated, m1 = tile(gates, t), keep1[pl.ds(HEAD + t, 1), :]
            state = [decay[n] * (state[n] * m1) + gated for n in range(modes)]
            rows_out[pl.ds(pl.multiple_of(t * pitch, pitch), pitch), :] = combine(
                [gain[n] * state[n] for n in range(modes)]
            )
        return state

    def send(slot, c, axis, me, count, step, send_sem, recv_sem):
        lower, size = pieces[c]
        piece = gathered.at[1 + slot, pl.ds(lower, size), :]
        return pltpu.make_async_remote_copy(
            src_ref=piece, dst_ref=piece, send_sem=send_sem, recv_sem=recv_sem,
            device_id={axis: lax.rem(me + step, count)}, device_id_type=MESH,
        )

    sent = []
    for c, (lower, size) in enumerate(pieces):
        carried = lax.fori_loop(lower // unroll, (lower + size) // unroll, advance, carried)

        def mix(r, carry):
            long_out = rows_out[pl.ds(lower * pitch + r, size, stride=pitch), :]
            gathered[1 + own, pl.ds(lower, size), lanes_of(r)] = (
                filtered(0, wide_q, r, lower, size) * long_out
            ).astype(BF16)
            return carry

        lax.fori_loop(0, rows, mix, 0)
        for step in range(1, grp):
            copy = send(own, c, "grp", g, grp, step, grp_send.at[step - 1, c], grp_recv.at[step - 1, c])
            copy.start()
            sent.append(copy)
        for step in range(1, sub):
            copy = send(own, c, "sub", s, sub, step, sub_send.at[step - 1, c], sub_recv.at[step - 1, c])
            copy.start()
            sent.append(copy)

    def product(slot, lower, count):
        depth = pl.ds(pl.multiple_of(slot * channels, channels), channels)
        return jnp.dot(
            gathered[1 + slot, pl.ds(lower, count), :], weight[depth, :], preferred_element_type=F32
        )

    load_weight.wait()
    total[...] = product(own, 0, tokens)
    for step in range(1, sub):
        slot = g * sub + lax.rem(s + sub - step, sub)
        for c in range(len(pieces)):
            send(slot, c, "sub", s, sub, step, sub_send.at[step - 1, c], sub_recv.at[step - 1, c]).wait_recv()
        total[...] += product(slot, 0, tokens)

    def extent(members):
        lower = pieces[members[0]][0]
        return lower, sum(pieces[c][1] for c in members)

    def finish(members):
        lower, count = extent(members)
        at = pl.ds(lower, count)
        for step in range(1, grp):
            source = lax.rem(g + grp - step, grp)
            for side in range(1, sub):
                slot = source * sub + lax.rem(s + sub - side, sub)
                for c in members:
                    sems = fwd_send.at[step - 1, side - 1, c], fwd_recv.at[step - 1, side - 1, c]
                    send(slot, c, "sub", s, sub, side, *sems).wait_recv()
                total[at, :] += product(slot, lower, count)
        out_ref[at, :] = total[at, :].astype(out_ref.dtype)

    for i, members in enumerate(groupings):
        lower, count = extent(members)
        for step in range(1, grp):
            slot = lax.rem(g + grp - step, grp) * sub + s
            for c in members:
                send(slot, c, "grp", g, grp, step, grp_send.at[step - 1, c], grp_recv.at[step - 1, c]).wait_recv()
                for side in range(1, sub):
                    sems = fwd_send.at[step - 1, side - 1, c], fwd_recv.at[step - 1, side - 1, c]
                    copy = send(slot, c, "sub", s, sub, side, *sems)
                    copy.start()
                    sent.append(copy)
            total[pl.ds(lower, count), :] += product(slot, lower, count)
        if i > 0:
            finish(groupings[i - 1])
    finish(groupings[-1])

    for copy in sent:
        copy.wait_send()
    pl.when(z < seq - 1)(send_halo.wait_send)
    for step in steps:
        pl.when(z + step < seq)(state_copies[step - 1].wait_send)


def shards(sizes, projected, short_filter, span_lengths, mode_rates, mode_residues, out_weight):
    seq, grp, sub = sizes
    tokens, _, channels = projected.shape
    modes, groups = mode_rates.shape
    rows = channels // LANES
    pitch = -(-rows // 8) * 8
    reach_steps = min(seq - 1, (seq * tokens // 2 - 1 + tokens - 1) // tokens)
    size = 32
    pieces = tuple((lower, size) for lower in range(0, tokens, size))
    count = len(pieces)
    groupings = tuple((i, i + 1) for i in range(0, count - 2, 2)) + ((count - 2,), (count - 1,))
    per_row = LANES * groups // channels
    streams = projected.transpose(1, 0, 2)
    vmem = pl.BlockSpec(memory_space=pltpu.VMEM)
    hbm = pl.BlockSpec(memory_space=pl.ANY)
    dma = pltpu.SemaphoreType.DMA
    row_tile = pltpu.VMEM((tokens * pitch, LANES), F32)
    stream = pltpu.VMEM((rows, tokens + HEAD, LANES), F32)
    state = (modes, channels)
    return pl.pallas_call(
        functools.partial(kernel, (seq, grp, sub, reach_steps, pieces, groupings)),
        out_shape=pltpu.VMEM((tokens, out_weight.shape[1]), BF16),
        in_specs=[hbm] * 6,
        out_specs=vmem,
        scratch_shapes=[
            pltpu.SMEM(span_lengths.shape, jnp.int32),
            pltpu.VMEM(streams.shape, BF16),
            pltpu.VMEM((3, EDGE, channels), BF16),
            pltpu.VMEM(short_filter.shape, F32),
            pltpu.VMEM(mode_rates.shape, F32),
            pltpu.VMEM(mode_residues.shape, F32),
            pltpu.VMEM(out_weight.shape, BF16),
            stream, stream, stream,
            pltpu.VMEM((tokens + HEAD, LANES), F32),
            pltpu.VMEM((tokens, LANES), F32),
            pltpu.VMEM((rows, 2 * per_row * modes, tokens), F32),
            pltpu.VMEM((2 * modes * pitch, LANES), F32),
            pltpu.VMEM(state, F32),
            row_tile, row_tile,
            pltpu.VMEM((8, LANES), F32),
            pltpu.VMEM((6 * pitch, LANES), F32),
            pltpu.VMEM((6 * pitch, LANES), BF16),
            pltpu.VMEM((6 * pitch, LANES), BF16),
            pltpu.VMEM(state, F32),
            pltpu.VMEM((reach_steps,) + state, F32),
            pltpu.VMEM((modes * pitch, LANES), F32),
            pltpu.VMEM((1 + grp * sub, tokens, channels), BF16),
            pltpu.VMEM((tokens, out_weight.shape[1]), F32),
            dma((7,)), dma, dma, dma,
            dma((reach_steps,)), dma((reach_steps,)),
            dma((sub - 1, count)), dma((sub - 1, count)),
            dma((grp - 1, count)), dma((grp - 1, count)),
            dma((grp - 1, sub - 1, count)), dma((grp - 1, sub - 1, count)),
        ],
        compiler_params=pltpu.CompilerParams(collective_id=0, has_side_effects=True),
    )(span_lengths, streams, short_filter, mode_rates, mode_residues, out_weight)


def solution(mesh):
    sizes = (mesh.shape["seq"], mesh.shape["grp"], mesh.shape["sub"])
    return jax.shard_map(
        functools.partial(shards, sizes),
        mesh=mesh,
        in_specs=(
            P(("parts", "seq"), None, ("grp", "sub")),
            P(None, None, ("grp", "sub")),
            P("parts"),
            P(None, ("grp", "sub")),
            P(None, ("grp", "sub")),
            P(None, ("grp", "sub")),
        ),
        out_specs=P(("parts", "seq"), ("grp", "sub")),
        check_vma=False,
    )
```

```python
import functools

import jax
import jax.numpy as jnp
from jax import lax
from jax.experimental import pallas as pl
from jax.experimental.pallas import tpu as pltpu
from jax.sharding import PartitionSpec as P

MESH = pl.DeviceIdType.MESH
LANES = 128
HEAD = 8
EDGE = 16
F32, BF16 = jnp.float32, jnp.bfloat16


def tanh(x):
    x = jnp.clip(x, -7.90531110763549805, 7.90531110763549805)
    square = x * x
    top = jnp.full_like(x, -2.76076847742355e-16)
    for c in (
        2.00018790482477e-13, -8.60467152213735e-11, 5.12229709037114e-08,
        1.48572235717979e-05, 6.37261928875436e-04, 4.89352455891786e-03,
    ):
        top = top * square + c
    bottom = jnp.full_like(x, 1.19825839466702e-06)
    for c in (1.18534705686654e-04, 2.26843463243900e-03, 4.89352518554385e-03):
        bottom = bottom * square + c
    return jnp.where(jnp.abs(x) < 0.0004, x, x * top / bottom)


def kernel(
    sizes, spans_hbm, x_hbm, taps_hbm, rates_hbm, residues_hbm, weight_hbm, out_ref,
    spans_ref, x_ref, edge_ref, taps_ref, rates_ref, residues_ref, weight,
    wide_q, wide_k, wide_v, keep1, keep2, powers, mode_rows, wide_rates, first_powers, partial,
    gates, rows_out, halo_rows, halo_out, halo_in, state_out, state_sent, state_in, incoming,
    gathered, total,
    load_sems, weight_sem, halo_send, halo_recv, state_send, state_recv,
    sub_send, sub_recv, grp_send, grp_recv, fwd_send, fwd_recv,
):
    seq, grp, sub, reach_steps, pieces, groupings = sizes
    _, tokens, channels = x_ref.shape
    modes, groups = rates_ref.shape
    rows = channels // LANES
    pitch = gates.shape[0] // tokens
    group_size = channels // groups
    per_row = LANES // group_size
    steps = range(1, reach_steps + 1)
    z, g, s = lax.axis_index("seq"), lax.axis_index("grp"), lax.axis_index("sub")
    offset = z * tokens

    loads = [
        pltpu.make_async_copy(source, target, load_sems.at[i])
        for i, (source, target) in enumerate((
            (rates_hbm, rates_ref), (residues_hbm, residues_ref), (spans_hbm, spans_ref),
            (x_hbm.at[:, pl.ds(tokens - EDGE, EDGE), :], edge_ref), (taps_hbm, taps_ref),
            (x_hbm.at[pl.ds(1, 2)], x_ref.at[pl.ds(1, 2)]), (x_hbm.at[pl.ds(0, 1)], x_ref.at[pl.ds(0, 1)]),
        ))
    ]
    load_rates, load_residues, load_spans, load_edge, load_taps, load_kv, load_q = loads
    for load in loads:
        load.start()

    barrier = pltpu.get_barrier_semaphore()
    for step in steps:
        @pl.when(z >= step)
        def _():
            pl.semaphore_signal(barrier, inc=1, device_id={"seq": z - step}, device_id_type=MESH)
    for axis, me, count in (("grp", g, grp), ("sub", s, sub)):
        for step in range(1, count):
            pl.semaphore_signal(
                barrier, inc=1, device_id={axis: lax.rem(me + step, count)}, device_id_type=MESH
            )
    load_weight = pltpu.make_async_copy(weight_hbm, weight, weight_sem)
    load_weight.start()

    if pitch != rows:
        for buffer in (gates, mode_rows):
            buffer[...] = jnp.zeros_like(buffer)
    incoming[...] = jnp.zeros_like(incoming)
    for buffer in (wide_k, wide_v):
        buffer[:, pl.ds(0, HEAD), :] = jnp.zeros((rows, HEAD, LANES), F32)

    load_spans.wait()
    starts, start = [], jnp.int32(0)
    for i in range(spans_ref.shape[0]):
        starts.append(start)
        start = start + spans_ref[i]
    latest = jnp.int32(0)
    for first in starts:
        latest = jnp.where(first < offset + tokens, first, latest)
    position = offset - HEAD + lax.broadcasted_iota(jnp.int32, (tokens + HEAD, LANES), 0)
    here = position == starts[0]
    for first in starts[1:]:
        here = here | (position == first)
    keep1[...] = jnp.where(here, 0.0, 1.0)
    keep2[...] = keep1[pl.ds(HEAD, tokens), :] * keep1[pl.ds(HEAD - 1, tokens), :]

    load_rates.wait()
    load_residues.wait()
    rates = rates_ref[...]
    token = lax.broadcasted_iota(jnp.int32, (modes, tokens), 1)
    ahead = (token - (tokens - 1)).astype(F32)
    live = jnp.where((offset + token >= latest) & (token >= 2), 1.0, 0.0)
    for c in range(rows):
        for i in range(per_row):
            rate = jnp.broadcast_to(rates[:, c * per_row + i : c * per_row + i + 1], (modes, tokens))
            power = jnp.exp(rate * ahead) * live
            high = power.astype(BF16).astype(F32)
            wide_at = pl.ds(i * modes, modes)
            powers[c, wide_at, :] = high
            powers[c, pl.ds((per_row + i) * modes, modes), :] = power - high

    spread = (
        lax.broadcasted_iota(jnp.int32, (groups, channels), 1) // group_size
        == lax.broadcasted_iota(jnp.int32, (groups, channels), 0)
    ).astype(F32)
    drop = tanh(rates) * (1.0 + jnp.exp(-2.0 * rates))
    for first, values in ((0, rates), (modes, residues_ref[...] * jnp.sqrt(drop))):
        wide = jnp.dot(values, spread, precision=lax.Precision.HIGHEST, preferred_element_type=F32)
        if first == 0:
            wide_rates[...] = wide
            for t in range(2):
                first_live = jnp.where(offset + t >= latest, 1.0, 0.0)
                first_powers[t] = jnp.exp(wide * (-float(tokens - 1 - t))) * first_live
        for c in range(rows):
            mode_rows[pl.ds(first * pitch + c, modes, stride=pitch), :] = wide[
                :, c * LANES : (c + 1) * LANES
            ]

    load_edge.wait()
    for j in range(3):
        for c in range(rows):
            lanes = slice(c * LANES, (c + 1) * LANES)
            halo_rows[pl.ds(2 * j * pitch + c, 2, stride=pitch), :] = edge_ref[j, :, lanes].astype(F32)[EDGE - 2 :]
    halo_out[...] = halo_rows[...].astype(BF16)

    load_taps.wait()

    def lanes_of(c):
        if isinstance(c, int):
            return slice(c * LANES, (c + 1) * LANES)
        return pl.ds(pl.multiple_of(c * LANES, LANES), LANES)

    def filtered(j, buffer, c, lower, count):
        tap = [taps_ref[k, pl.ds(j, 1), lanes_of(c)] for k in range(3)]
        now, last, older = (buffer[c, pl.ds(HEAD + lower - k, count), :] for k in range(3))
        m1, m2 = keep1[pl.ds(HEAD + lower, count), :], keep2[pl.ds(lower, count), :]
        return tap[0] * now + tap[1] * last * m1 + tap[2] * older * m2

    def gate(c, lower, count):
        value = (filtered(1, wide_k, c, lower, count) * filtered(2, wide_v, c, lower, count)).astype(BF16)
        gathered[0, pl.ds(lower, count), lanes_of(c)] = value
        gates[pl.ds(lower * pitch + c, count, stride=pitch), :] = value.astype(F32)

    load_kv.wait()
    block = 64

    def gate_rows(c, carry):
        for j, buffer in ((1, wide_k), (2, wide_v)):
            buffer[c, pl.ds(HEAD, tokens), :] = x_ref[j, :, lanes_of(c)].astype(F32)
        lower = 0
        while lower < tokens:
            count = min(block, tokens - lower)
            gate(c, lower, count)
            lower += count
        return carry

    lax.fori_loop(0, rows, gate_rows, 0)

    lane_group = lax.broadcasted_iota(jnp.int32, (modes, LANES), 1) // group_size
    for c in range(rows):
        lanes = slice(c * LANES, (c + 1) * LANES)
        sums = jnp.dot(powers[c].astype(BF16), gathered[0, :, lanes], preferred_element_type=F32)
        sums = sums[: per_row * modes] + sums[per_row * modes :]
        state = sums[:modes]
        for i in range(1, per_row):
            state = jnp.where(lane_group == i, sums[i * modes : (i + 1) * modes], state)
        partial[:, lanes] = state

    pl.semaphore_wait(barrier, jnp.minimum(reach_steps, seq - 1 - z) + grp + sub - 2)

    send_halo = pltpu.make_async_remote_copy(
        src_ref=halo_out, dst_ref=halo_in, send_sem=halo_send, recv_sem=halo_recv,
        device_id={"seq": lax.rem(z + 1, seq)}, device_id_type=MESH,
    )

    @pl.when(z < seq - 1)
    def _():
        send_halo.start()

    @pl.when(z == 0)
    def _():
        halo_in[...] = jnp.zeros_like(halo_in)

    @pl.when(z > 0)
    def _():
        send_halo.wait_recv()

    halo_rows[...] = halo_in[...].astype(F32)
    for j, buffer in enumerate((wide_q, wide_k, wide_v)):
        for c in range(rows):
            buffer[c, pl.ds(HEAD - 2, 2), :] = halo_rows[pl.ds(2 * j * pitch + c, 2, stride=pitch), :]
    for c in range(rows):
        lanes = slice(c * LANES, (c + 1) * LANES)
        value = filtered(1, wide_k, c, 0, HEAD) * filtered(2, wide_v, c, 0, HEAD)
        value = value.astype(BF16).astype(F32)
        gates[pl.ds(c, HEAD, stride=pitch), :] = value
        state = partial[:, lanes] + first_powers[0, :, lanes] * value[0:1] + first_powers[1, :, lanes] * value[1:2]
        half = c * 2 // rows
        state_out[pl.ds(half * modes, modes), slice((c - half * rows // 2) * LANES, (c - half * rows // 2 + 1) * LANES)] = state

    state_sent[...] = state_out[...].astype(BF16)
    state_copies = []
    for step in steps:
        copy = pltpu.make_async_remote_copy(
            src_ref=state_sent, dst_ref=state_in.at[step - 1],
            send_sem=state_send.at[step - 1], recv_sem=state_recv.at[step - 1],
            device_id={"seq": lax.rem(z + step, seq)}, device_id_type=MESH,
        )
        state_copies.append(copy)
    for step in reversed(steps):
        pl.when(z + step < seq)(state_copies[step - 1].start)

    def tile(ref, index):
        return ref[pl.ds(pl.multiple_of(index * pitch, pitch), pitch), :]

    decay = [jnp.exp(-tile(mode_rows, n)) for n in range(modes)]
    gain = [tile(mode_rows, modes + n) for n in range(modes)]
    load_q.wait()

    for step in steps:
        reach = (step - 1) * tokens
        open_ = jnp.float32(1.0)
        for first in starts:
            inside = (first >= offset - reach) & (first <= offset - 1)
            open_ = jnp.where(inside, 0.0, open_)

        @pl.when(z >= step)
        def _():
            state_copies[step - 1].wait_recv()
            came = state_in[step - 1].astype(F32)
            for c in range(rows):
                lanes = slice(c * LANES, (c + 1) * LANES)
                half = c * 2 // rows
                left = (c - half * rows // 2) * LANES
                part = came[half * modes : (half + 1) * modes, left : left + LANES] * open_
                if reach:
                    part = part * jnp.exp(wide_rates[:, lanes] * (-float(reach)))
                at = pl.ds(c, modes, stride=pitch)
                incoming[at, :] = incoming[at, :] + part

    own = g * sub + s
    carried = [tile(incoming, n) for n in range(modes)]
    unroll = 8

    def combine(parts):
        while len(parts) > 1:
            parts = [sum(parts[i + 1 : i + 2], parts[i]) for i in range(0, len(parts), 2)]
        return parts[0]

    def advance(block, state):
        for u in range(unroll):
            t = block * unroll + u
            gated, m1 = tile(gates, t), keep1[pl.ds(HEAD + t, 1), :]
            state = [decay[n] * (state[n] * m1) + gated for n in range(modes)]
            rows_out[pl.ds(pl.multiple_of(t * pitch, pitch), pitch), :] = combine(
                [gain[n] * state[n] for n in range(modes)]
            )
        return state

    def send(slot, c, axis, me, count, step, send_sem, recv_sem):
        lower, size = pieces[c]
        piece = gathered.at[1 + slot, pl.ds(lower, size), :]
        return pltpu.make_async_remote_copy(
            src_ref=piece, dst_ref=piece, send_sem=send_sem, recv_sem=recv_sem,
            device_id={axis: lax.rem(me + step, count)}, device_id_type=MESH,
        )

    sent = []
    for c, (lower, size) in enumerate(pieces):
        carried = lax.fori_loop(lower // unroll, (lower + size) // unroll, advance, carried)

        def mix(r, carry):
            wide_q[r, pl.ds(HEAD + lower, size), :] = x_ref[0, pl.ds(lower, size), lanes_of(r)].astype(F32)
            long_out = rows_out[pl.ds(lower * pitch + r, size, stride=pitch), :]
            gathered[1 + own, pl.ds(lower, size), lanes_of(r)] = (
                filtered(0, wide_q, r, lower, size) * long_out
            ).astype(BF16)
            return carry

        lax.fori_loop(0, rows, mix, 0)
        for step in range(1, grp):
            copy = send(own, c, "grp", g, grp, step, grp_send.at[step - 1, c], grp_recv.at[step - 1, c])
            copy.start()
            sent.append(copy)
        for step in range(1, sub):
            copy = send(own, c, "sub", s, sub, step, sub_send.at[step - 1, c], sub_recv.at[step - 1, c])
            copy.start()
            sent.append(copy)

    def product(slot, lower, count):
        depth = pl.ds(pl.multiple_of(slot * channels, channels), channels)
        return jnp.dot(
            gathered[1 + slot, pl.ds(lower, count), :], weight[depth, :], preferred_element_type=F32
        )

    load_weight.wait()
    total[...] = product(own, 0, tokens)
    for step in range(1, sub):
        slot = g * sub + lax.rem(s + sub - step, sub)
        for c in range(len(pieces)):
            send(slot, c, "sub", s, sub, step, sub_send.at[step - 1, c], sub_recv.at[step - 1, c]).wait_recv()
        total[...] += product(slot, 0, tokens)

    def extent(members):
        lower = pieces[members[0]][0]
        return lower, sum(pieces[c][1] for c in members)

    def finish(members):
        lower, count = extent(members)
        at = pl.ds(lower, count)
        for step in range(1, grp):
            source = lax.rem(g + grp - step, grp)
            for side in range(1, sub):
                slot = source * sub + lax.rem(s + sub - side, sub)
                for c in members:
                    sems = fwd_send.at[step - 1, side - 1, c], fwd_recv.at[step - 1, side - 1, c]
                    send(slot, c, "sub", s, sub, side, *sems).wait_recv()
                total[at, :] += product(slot, lower, count)
        out_ref[at, :] = total[at, :].astype(out_ref.dtype)

    for i, members in enumerate(groupings):
        lower, count = extent(members)
        for step in range(1, grp):
            slot = lax.rem(g + grp - step, grp) * sub + s
            for c in members:
                send(slot, c, "grp", g, grp, step, grp_send.at[step - 1, c], grp_recv.at[step - 1, c]).wait_recv()
                for side in range(1, sub):
                    sems = fwd_send.at[step - 1, side - 1, c], fwd_recv.at[step - 1, side - 1, c]
                    copy = send(slot, c, "sub", s, sub, side, *sems)
                    copy.start()
                    sent.append(copy)
            total[pl.ds(lower, count), :] += product(slot, lower, count)
        if i > 0:
            finish(groupings[i - 1])
    finish(groupings[-1])

    for copy in sent:
        copy.wait_send()
    pl.when(z < seq - 1)(send_halo.wait_send)
    for step in steps:
        pl.when(z + step < seq)(state_copies[step - 1].wait_send)


def shards(sizes, projected, short_filter, span_lengths, mode_rates, mode_residues, out_weight):
    seq, grp, sub = sizes
    tokens, _, channels = projected.shape
    modes, groups = mode_rates.shape
    rows = channels // LANES
    pitch = -(-rows // 8) * 8
    reach_steps = min(seq - 1, (seq * tokens // 2 - 1 + tokens - 1) // tokens)
    sizes_of = (16, 16) + (32,) * ((tokens - 64) // 32) + (16, 16)
    pieces = tuple((sum(sizes_of[:i]), size) for i, size in enumerate(sizes_of))
    count = len(pieces)
    groupings = ((0, 1, 2),) + tuple((i, i + 1) for i in range(3, count - 3, 2)) + ((count - 3,), (count - 2,), (count - 1,))
    per_row = LANES * groups // channels
    streams = projected.transpose(1, 0, 2)
    vmem = pl.BlockSpec(memory_space=pltpu.VMEM)
    hbm = pl.BlockSpec(memory_space=pl.ANY)
    dma = pltpu.SemaphoreType.DMA
    row_tile = pltpu.VMEM((tokens * pitch, LANES), F32)
    stream = pltpu.VMEM((rows, tokens + HEAD, LANES), F32)
    state, packed = (modes, channels), (2 * modes, channels // 2)
    return pl.pallas_call(
        functools.partial(kernel, (seq, grp, sub, reach_steps, pieces, groupings)),
        out_shape=pltpu.VMEM((tokens, out_weight.shape[1]), BF16),
        in_specs=[hbm] * 6,
        out_specs=vmem,
        scratch_shapes=[
            pltpu.SMEM(span_lengths.shape, jnp.int32),
            pltpu.VMEM(streams.shape, BF16),
            pltpu.VMEM((3, EDGE, channels), BF16),
            pltpu.VMEM(short_filter.shape, F32),
            pltpu.VMEM(mode_rates.shape, F32),
            pltpu.VMEM(mode_residues.shape, F32),
            pltpu.VMEM(out_weight.shape, BF16),
            stream, stream, stream,
            pltpu.VMEM((tokens + HEAD, LANES), F32),
            pltpu.VMEM((tokens, LANES), F32),
            pltpu.VMEM((rows, 2 * per_row * modes, tokens), F32),
            pltpu.VMEM((2 * modes * pitch, LANES), F32),
            pltpu.VMEM(state, F32),
            pltpu.VMEM((2,) + state, F32),
            pltpu.VMEM(state, F32),
            row_tile, row_tile,
            pltpu.VMEM((6 * pitch, LANES), F32),
            pltpu.VMEM((6 * pitch, LANES), BF16),
            pltpu.VMEM((6 * pitch, LANES), BF16),
            pltpu.VMEM(packed, F32),
            pltpu.VMEM(packed, BF16),
            pltpu.VMEM((reach_steps,) + packed, BF16),
            pltpu.VMEM((modes * pitch, LANES), F32),
            pltpu.VMEM((1 + grp * sub, tokens, channels), BF16),
            pltpu.VMEM((tokens, out_weight.shape[1]), F32),
            dma((7,)), dma, dma, dma,
            dma((reach_steps,)), dma((reach_steps,)),
            dma((sub - 1, count)), dma((sub - 1, count)),
            dma((grp - 1, count)), dma((grp - 1, count)),
            dma((grp - 1, sub - 1, count)), dma((grp - 1, sub - 1, count)),
        ],
        compiler_params=pltpu.CompilerParams(collective_id=0, has_side_effects=True),
    )(span_lengths, streams, short_filter, mode_rates, mode_residues, out_weight)


def solution(mesh):
    sizes = (mesh.shape["seq"], mesh.shape["grp"], mesh.shape["sub"])
    return jax.shard_map(
        functools.partial(shards, sizes),
        mesh=mesh,
        in_specs=(
            P(("parts", "seq"), None, ("grp", "sub")),
            P(None, None, ("grp", "sub")),
            P("parts"),
            P(None, ("grp", "sub")),
            P(None, ("grp", "sub")),
            P(None, ("grp", "sub")),
        ),
        out_specs=P(("parts", "seq"), ("grp", "sub")),
        check_vma=False,
    )
```

```python
import functools

import jax
import jax.numpy as jnp
from jax import lax
from jax.experimental import pallas as pl
from jax.experimental.pallas import tpu as pltpu
from jax.sharding import PartitionSpec as P

MESH = pl.DeviceIdType.MESH
LANES = 128
HEAD = 8
EDGE = 16
F32, BF16 = jnp.float32, jnp.bfloat16


def tanh(x):
    x = jnp.clip(x, -7.90531110763549805, 7.90531110763549805)
    square = x * x
    top = jnp.full_like(x, -2.76076847742355e-16)
    for c in (
        2.00018790482477e-13, -8.60467152213735e-11, 5.12229709037114e-08,
        1.48572235717979e-05, 6.37261928875436e-04, 4.89352455891786e-03,
    ):
        top = top * square + c
    bottom = jnp.full_like(x, 1.19825839466702e-06)
    for c in (1.18534705686654e-04, 2.26843463243900e-03, 4.89352518554385e-03):
        bottom = bottom * square + c
    return jnp.where(jnp.abs(x) < 0.0004, x, x * top / bottom)


def kernel(
    sizes, spans_hbm, x_hbm, taps_hbm, rates_hbm, residues_hbm, weight_hbm, out_ref,
    spans_ref, x_ref, edge_ref, taps_ref, rates_ref, residues_ref, weight,
    wide_q, wide_k, wide_v, keep1, keep2, powers, mode_rows, wide_rates, first_powers, partial,
    gates, rows_out, halo_rows, halo_out, halo_in, state_out, state_sent, state_in, incoming,
    gathered, total,
    load_sems, weight_sem, halo_send, halo_recv, state_send, state_recv,
    sub_send, sub_recv, grp_send, grp_recv, fwd_send, fwd_recv,
):
    seq, grp, sub, reach_steps, pieces, groupings = sizes
    _, tokens, channels = x_ref.shape
    modes, groups = rates_ref.shape
    rows = channels // LANES
    pitch = gates.shape[0] // tokens
    group_size = channels // groups
    per_row = LANES // group_size
    steps = range(1, reach_steps + 1)
    z, g, s = lax.axis_index("seq"), lax.axis_index("grp"), lax.axis_index("sub")
    offset = z * tokens

    loads = [
        pltpu.make_async_copy(source, target, load_sems.at[i])
        for i, (source, target) in enumerate((
            (rates_hbm, rates_ref), (residues_hbm, residues_ref), (spans_hbm, spans_ref),
            (x_hbm.at[:, pl.ds(tokens - EDGE, EDGE), :], edge_ref), (taps_hbm, taps_ref),
            (x_hbm.at[pl.ds(1, 2)], x_ref.at[pl.ds(1, 2)]), (x_hbm.at[pl.ds(0, 1)], x_ref.at[pl.ds(0, 1)]),
        ))
    ]
    load_rates, load_residues, load_spans, load_edge, load_taps, load_kv, load_q = loads
    for load in loads:
        load.start()

    barrier = pltpu.get_barrier_semaphore()
    for step in steps:
        @pl.when(z >= step)
        def _():
            pl.semaphore_signal(barrier, inc=1, device_id={"seq": z - step}, device_id_type=MESH)
    for axis, me, count in (("grp", g, grp), ("sub", s, sub)):
        for step in range(1, count):
            pl.semaphore_signal(
                barrier, inc=1, device_id={axis: lax.rem(me + step, count)}, device_id_type=MESH
            )
    load_weight = pltpu.make_async_copy(weight_hbm, weight, weight_sem)
    load_weight.start()

    if pitch != rows:
        for buffer in (gates, mode_rows):
            buffer[...] = jnp.zeros_like(buffer)
    incoming[...] = jnp.zeros_like(incoming)
    for buffer in (wide_k, wide_v):
        buffer[:, pl.ds(0, HEAD), :] = jnp.zeros((rows, HEAD, LANES), F32)

    load_spans.wait()
    starts, start = [], jnp.int32(0)
    for i in range(spans_ref.shape[0]):
        starts.append(start)
        start = start + spans_ref[i]
    latest = jnp.int32(0)
    for first in starts:
        latest = jnp.where(first < offset + tokens, first, latest)
    position = offset - HEAD + lax.broadcasted_iota(jnp.int32, (tokens + HEAD, LANES), 0)
    here = position == starts[0]
    for first in starts[1:]:
        here = here | (position == first)
    keep1[...] = jnp.where(here, 0.0, 1.0)
    keep2[...] = keep1[pl.ds(HEAD, tokens), :] * keep1[pl.ds(HEAD - 1, tokens), :]

    load_rates.wait()
    load_residues.wait()
    rates = rates_ref[...]
    token = lax.broadcasted_iota(jnp.int32, (modes, tokens), 1)
    ahead = (token - (tokens - 1)).astype(F32)
    live = jnp.where((offset + token >= latest) & (token >= 2), 1.0, 0.0)
    for c in range(rows):
        for i in range(per_row):
            rate = jnp.broadcast_to(rates[:, c * per_row + i : c * per_row + i + 1], (modes, tokens))
            power = jnp.exp(rate * ahead) * live
            high = power.astype(BF16).astype(F32)
            wide_at = pl.ds(i * modes, modes)
            powers[c, wide_at, :] = high
            powers[c, pl.ds((per_row + i) * modes, modes), :] = power - high

    spread = (
        lax.broadcasted_iota(jnp.int32, (groups, channels), 1) // group_size
        == lax.broadcasted_iota(jnp.int32, (groups, channels), 0)
    ).astype(F32)
    drop = tanh(rates) * (1.0 + jnp.exp(-2.0 * rates))
    for first, values in ((0, rates), (modes, residues_ref[...] * jnp.sqrt(drop))):
        wide = jnp.dot(values, spread, precision=lax.Precision.HIGHEST, preferred_element_type=F32)
        if first == 0:
            wide_rates[...] = wide
            for t in range(2):
                first_live = jnp.where(offset + t >= latest, 1.0, 0.0)
                first_powers[t] = jnp.exp(wide * (-float(tokens - 1 - t))) * first_live
        for c in range(rows):
            mode_rows[pl.ds(first * pitch + c, modes, stride=pitch), :] = wide[
                :, c * LANES : (c + 1) * LANES
            ]

    load_edge.wait()
    for j in range(3):
        for c in range(rows):
            lanes = slice(c * LANES, (c + 1) * LANES)
            halo_rows[pl.ds(2 * j * pitch + c, 2, stride=pitch), :] = edge_ref[j, :, lanes].astype(F32)[EDGE - 2 :]
    halo_out[...] = halo_rows[...].astype(BF16)

    load_taps.wait()

    def lanes_of(c):
        if isinstance(c, int):
            return slice(c * LANES, (c + 1) * LANES)
        return pl.ds(pl.multiple_of(c * LANES, LANES), LANES)

    def filtered(j, buffer, c, lower, count):
        tap = [taps_ref[k, pl.ds(j, 1), lanes_of(c)] for k in range(3)]
        now, last, older = (buffer[c, pl.ds(HEAD + lower - k, count), :] for k in range(3))
        m1, m2 = keep1[pl.ds(HEAD + lower, count), :], keep2[pl.ds(lower, count), :]
        return tap[0] * now + tap[1] * last * m1 + tap[2] * older * m2

    def gate(c, lower, count):
        value = (filtered(1, wide_k, c, lower, count) * filtered(2, wide_v, c, lower, count)).astype(BF16)
        gathered[0, pl.ds(lower, count), lanes_of(c)] = value
        gates[pl.ds(lower * pitch + c, count, stride=pitch), :] = value.astype(F32)

    load_kv.wait()
    block = 64

    def gate_rows(c, carry):
        for j, buffer in ((1, wide_k), (2, wide_v)):
            buffer[c, pl.ds(HEAD, tokens), :] = x_ref[j, :, lanes_of(c)].astype(F32)
        lower = 0
        while lower < tokens:
            count = min(block, tokens - lower)
            gate(c, lower, count)
            lower += count
        return carry

    lax.fori_loop(0, rows, gate_rows, 0)

    pl.semaphore_wait(barrier, jnp.minimum(reach_steps, seq - 1 - z) + grp + sub - 2)

    send_halo = pltpu.make_async_remote_copy(
        src_ref=halo_out, dst_ref=halo_in, send_sem=halo_send, recv_sem=halo_recv,
        device_id={"seq": lax.rem(z + 1, seq)}, device_id_type=MESH,
    )

    @pl.when(z < seq - 1)
    def _():
        send_halo.start()

    lane_group = lax.broadcasted_iota(jnp.int32, (modes, LANES), 1) // group_size
    for c in range(rows):
        lanes = slice(c * LANES, (c + 1) * LANES)
        sums = jnp.dot(powers[c].astype(BF16), gathered[0, :, lanes], preferred_element_type=F32)
        sums = sums[: per_row * modes] + sums[per_row * modes :]
        state = sums[:modes]
        for i in range(1, per_row):
            state = jnp.where(lane_group == i, sums[i * modes : (i + 1) * modes], state)
        partial[:, lanes] = state

    @pl.when(z == 0)
    def _():
        halo_in[...] = jnp.zeros_like(halo_in)

    @pl.when(z > 0)
    def _():
        send_halo.wait_recv()

    halo_rows[...] = halo_in[...].astype(F32)
    for j, buffer in enumerate((wide_q, wide_k, wide_v)):
        for c in range(rows):
            buffer[c, pl.ds(HEAD - 2, 2), :] = halo_rows[pl.ds(2 * j * pitch + c, 2, stride=pitch), :]
    for c in range(rows):
        lanes = slice(c * LANES, (c + 1) * LANES)
        value = filtered(1, wide_k, c, 0, HEAD) * filtered(2, wide_v, c, 0, HEAD)
        value = value.astype(BF16).astype(F32)
        gates[pl.ds(c, HEAD, stride=pitch), :] = value
        state = partial[:, lanes] + first_powers[0, :, lanes] * value[0:1] + first_powers[1, :, lanes] * value[1:2]
        half = c * 2 // rows
        state_out[pl.ds(half * modes, modes), slice((c - half * rows // 2) * LANES, (c - half * rows // 2 + 1) * LANES)] = state

    state_sent[...] = state_out[...].astype(BF16)
    state_copies = []
    for step in steps:
        copy = pltpu.make_async_remote_copy(
            src_ref=state_sent, dst_ref=state_in.at[step - 1],
            send_sem=state_send.at[step - 1], recv_sem=state_recv.at[step - 1],
            device_id={"seq": lax.rem(z + step, seq)}, device_id_type=MESH,
        )
        state_copies.append(copy)
    for step in reversed(steps):
        pl.when(z + step < seq)(state_copies[step - 1].start)

    def tile(ref, index):
        return ref[pl.ds(pl.multiple_of(index * pitch, pitch), pitch), :]

    decay = [jnp.exp(-tile(mode_rows, n)) for n in range(modes)]
    gain = [tile(mode_rows, modes + n) for n in range(modes)]
    load_q.wait()

    for step in steps:
        reach = (step - 1) * tokens
        open_ = jnp.float32(1.0)
        for first in starts:
            inside = (first >= offset - reach) & (first <= offset - 1)
            open_ = jnp.where(inside, 0.0, open_)

        @pl.when(z >= step)
        def _():
            state_copies[step - 1].wait_recv()
            came = state_in[step - 1].astype(F32)
            for c in range(rows):
                lanes = slice(c * LANES, (c + 1) * LANES)
                half = c * 2 // rows
                left = (c - half * rows // 2) * LANES
                part = came[half * modes : (half + 1) * modes, left : left + LANES] * open_
                if reach:
                    part = part * jnp.exp(wide_rates[:, lanes] * (-float(reach)))
                at = pl.ds(c, modes, stride=pitch)
                incoming[at, :] = incoming[at, :] + part

    own = g * sub + s
    carried = [tile(incoming, n) for n in range(modes)]
    unroll = 8

    def combine(parts):
        while len(parts) > 1:
            parts = [sum(parts[i + 1 : i + 2], parts[i]) for i in range(0, len(parts), 2)]
        return parts[0]

    def advance(block, state):
        for u in range(unroll):
            t = block * unroll + u
            gated, m1 = tile(gates, t), keep1[pl.ds(HEAD + t, 1), :]
            state = [decay[n] * (state[n] * m1) + gated for n in range(modes)]
            rows_out[pl.ds(pl.multiple_of(t * pitch, pitch), pitch), :] = combine(
                [gain[n] * state[n] for n in range(modes)]
            )
        return state

    def send(slot, c, axis, me, count, step, send_sem, recv_sem):
        lower, size = pieces[c]
        piece = gathered.at[1 + slot, pl.ds(lower, size), :]
        return pltpu.make_async_remote_copy(
            src_ref=piece, dst_ref=piece, send_sem=send_sem, recv_sem=recv_sem,
            device_id={axis: lax.rem(me + step, count)}, device_id_type=MESH,
        )

    sent = []
    for c, (lower, size) in enumerate(pieces):
        carried = lax.fori_loop(lower // unroll, (lower + size) // unroll, advance, carried)

        def mix(r, carry):
            wide_q[r, pl.ds(HEAD + lower, size), :] = x_ref[0, pl.ds(lower, size), lanes_of(r)].astype(F32)
            long_out = rows_out[pl.ds(lower * pitch + r, size, stride=pitch), :]
            gathered[1 + own, pl.ds(lower, size), lanes_of(r)] = (
                filtered(0, wide_q, r, lower, size) * long_out
            ).astype(BF16)
            return carry

        lax.fori_loop(0, rows, mix, 0)
        for step in range(1, grp):
            copy = send(own, c, "grp", g, grp, step, grp_send.at[step - 1, c], grp_recv.at[step - 1, c])
            copy.start()
            sent.append(copy)
        for step in range(1, sub):
            copy = send(own, c, "sub", s, sub, step, sub_send.at[step - 1, c], sub_recv.at[step - 1, c])
            copy.start()
            sent.append(copy)

    def product(slot, lower, count):
        depth = pl.ds(pl.multiple_of(slot * channels, channels), channels)
        return jnp.dot(
            gathered[1 + slot, pl.ds(lower, count), :], weight[depth, :], preferred_element_type=F32
        )

    load_weight.wait()
    total[...] = product(own, 0, tokens)
    for step in range(1, sub):
        slot = g * sub + lax.rem(s + sub - step, sub)
        for c in range(len(pieces)):
            send(slot, c, "sub", s, sub, step, sub_send.at[step - 1, c], sub_recv.at[step - 1, c]).wait_recv()
        total[...] += product(slot, 0, tokens)

    def extent(members):
        lower = pieces[members[0]][0]
        return lower, sum(pieces[c][1] for c in members)

    def finish(members):
        lower, count = extent(members)
        at = pl.ds(lower, count)
        for step in range(1, grp):
            source = lax.rem(g + grp - step, grp)
            for side in range(1, sub):
                slot = source * sub + lax.rem(s + sub - side, sub)
                for c in members:
                    sems = fwd_send.at[step - 1, side - 1, c], fwd_recv.at[step - 1, side - 1, c]
                    send(slot, c, "sub", s, sub, side, *sems).wait_recv()
                total[at, :] += product(slot, lower, count)
        out_ref[at, :] = total[at, :].astype(out_ref.dtype)

    for i, members in enumerate(groupings):
        lower, count = extent(members)
        for step in range(1, grp):
            slot = lax.rem(g + grp - step, grp) * sub + s
            for c in members:
                send(slot, c, "grp", g, grp, step, grp_send.at[step - 1, c], grp_recv.at[step - 1, c]).wait_recv()
                for side in range(1, sub):
                    sems = fwd_send.at[step - 1, side - 1, c], fwd_recv.at[step - 1, side - 1, c]
                    copy = send(slot, c, "sub", s, sub, side, *sems)
                    copy.start()
                    sent.append(copy)
            total[pl.ds(lower, count), :] += product(slot, lower, count)
        if i > 0:
            finish(groupings[i - 1])
    finish(groupings[-1])

    for copy in sent:
        copy.wait_send()
    pl.when(z < seq - 1)(send_halo.wait_send)
    for step in steps:
        pl.when(z + step < seq)(state_copies[step - 1].wait_send)


def shards(sizes, projected, short_filter, span_lengths, mode_rates, mode_residues, out_weight):
    seq, grp, sub = sizes
    tokens, _, channels = projected.shape
    modes, groups = mode_rates.shape
    rows = channels // LANES
    pitch = -(-rows // 8) * 8
    reach_steps = min(seq - 1, (seq * tokens // 2 - 1 + tokens - 1) // tokens)
    sizes_of = (16, 16) + (32,) * ((tokens - 64) // 32) + (16, 16)
    pieces = tuple((sum(sizes_of[:i]), size) for i, size in enumerate(sizes_of))
    count = len(pieces)
    groupings = (tuple(range(count - 5)), (count - 5, count - 4), (count - 3, count - 2), (count - 1,))
    per_row = LANES * groups // channels
    streams = projected.transpose(1, 0, 2)
    vmem = pl.BlockSpec(memory_space=pltpu.VMEM)
    hbm = pl.BlockSpec(memory_space=pl.ANY)
    dma = pltpu.SemaphoreType.DMA
    row_tile = pltpu.VMEM((tokens * pitch, LANES), F32)
    stream = pltpu.VMEM((rows, tokens + HEAD, LANES), F32)
    state, packed = (modes, channels), (2 * modes, channels // 2)
    return pl.pallas_call(
        functools.partial(kernel, (seq, grp, sub, reach_steps, pieces, groupings)),
        out_shape=pltpu.VMEM((tokens, out_weight.shape[1]), BF16),
        in_specs=[hbm] * 6,
        out_specs=vmem,
        scratch_shapes=[
            pltpu.SMEM(span_lengths.shape, jnp.int32),
            pltpu.VMEM(streams.shape, BF16),
            pltpu.VMEM((3, EDGE, channels), BF16),
            pltpu.VMEM(short_filter.shape, F32),
            pltpu.VMEM(mode_rates.shape, F32),
            pltpu.VMEM(mode_residues.shape, F32),
            pltpu.VMEM(out_weight.shape, BF16),
            stream, stream, stream,
            pltpu.VMEM((tokens + HEAD, LANES), F32),
            pltpu.VMEM((tokens, LANES), F32),
            pltpu.VMEM((rows, 2 * per_row * modes, tokens), F32),
            pltpu.VMEM((2 * modes * pitch, LANES), F32),
            pltpu.VMEM(state, F32),
            pltpu.VMEM((2,) + state, F32),
            pltpu.VMEM(state, F32),
            row_tile, row_tile,
            pltpu.VMEM((6 * pitch, LANES), F32),
            pltpu.VMEM((6 * pitch, LANES), BF16),
            pltpu.VMEM((6 * pitch, LANES), BF16),
            pltpu.VMEM(packed, F32),
            pltpu.VMEM(packed, BF16),
            pltpu.VMEM((reach_steps,) + packed, BF16),
            pltpu.VMEM((modes * pitch, LANES), F32),
            pltpu.VMEM((1 + grp * sub, tokens, channels), BF16),
            pltpu.VMEM((tokens, out_weight.shape[1]), F32),
            dma((7,)), dma, dma, dma,
            dma((reach_steps,)), dma((reach_steps,)),
            dma((sub - 1, count)), dma((sub - 1, count)),
            dma((grp - 1, count)), dma((grp - 1, count)),
            dma((grp - 1, sub - 1, count)), dma((grp - 1, sub - 1, count)),
        ],
        compiler_params=pltpu.CompilerParams(collective_id=0, has_side_effects=True),
    )(span_lengths, streams, short_filter, mode_rates, mode_residues, out_weight)


def solution(mesh):
    sizes = (mesh.shape["seq"], mesh.shape["grp"], mesh.shape["sub"])
    return jax.shard_map(
        functools.partial(shards, sizes),
        mesh=mesh,
        in_specs=(
            P(("parts", "seq"), None, ("grp", "sub")),
            P(None, None, ("grp", "sub")),
            P("parts"),
            P(None, ("grp", "sub")),
            P(None, ("grp", "sub")),
            P(None, ("grp", "sub")),
        ),
        out_specs=P(("parts", "seq"), ("grp", "sub")),
        check_vma=False,
    )
```

```python
import functools

import jax
import jax.numpy as jnp
from jax import lax
from jax.experimental import pallas as pl
from jax.experimental.pallas import tpu as pltpu
from jax.sharding import PartitionSpec as P

MESH = pl.DeviceIdType.MESH
LANES = 128
HEAD = 8
EDGE = 16
F32, BF16 = jnp.float32, jnp.bfloat16


def tanh(x):
    x = jnp.clip(x, -7.90531110763549805, 7.90531110763549805)
    square = x * x
    top = jnp.full_like(x, -2.76076847742355e-16)
    for c in (
        2.00018790482477e-13, -8.60467152213735e-11, 5.12229709037114e-08,
        1.48572235717979e-05, 6.37261928875436e-04, 4.89352455891786e-03,
    ):
        top = top * square + c
    bottom = jnp.full_like(x, 1.19825839466702e-06)
    for c in (1.18534705686654e-04, 2.26843463243900e-03, 4.89352518554385e-03):
        bottom = bottom * square + c
    return jnp.where(jnp.abs(x) < 0.0004, x, x * top / bottom)


def kernel(
    sizes, spans_hbm, x_hbm, taps_hbm, rates_hbm, residues_hbm, weight_hbm, out_ref,
    spans_ref, x_ref, edge_ref, taps_ref, rates_ref, residues_ref, weight,
    wide_q, wide_k, wide_v, keep1, keep2, powers, mode_rows, wide_rates, first_powers, partial,
    gates, rows_out, halo_rows, halo_out, halo_in, state_out, state_sent, state_in, incoming,
    gathered, total,
    load_sems, weight_sem, halo_send, halo_recv, state_send, state_recv,
    sub_send, sub_recv, grp_send, grp_recv, fwd_send, fwd_recv,
):
    seq, grp, sub, reach_steps, pieces, groupings, trigger = sizes
    _, tokens, channels = x_ref.shape
    modes, groups = rates_ref.shape
    held = len(pieces) - 1
    rows = channels // LANES
    pitch = gates.shape[0] // tokens
    group_size = channels // groups
    per_row = LANES // group_size
    steps = range(1, reach_steps + 1)
    z, g, s = lax.axis_index("seq"), lax.axis_index("grp"), lax.axis_index("sub")
    offset = z * tokens

    loads = [
        pltpu.make_async_copy(source, target, load_sems.at[i])
        for i, (source, target) in enumerate((
            (rates_hbm, rates_ref), (residues_hbm, residues_ref), (spans_hbm, spans_ref),
            (x_hbm.at[:, pl.ds(tokens - EDGE, EDGE), :], edge_ref), (taps_hbm, taps_ref),
            (x_hbm.at[pl.ds(1, 2)], x_ref.at[pl.ds(1, 2)]), (x_hbm.at[pl.ds(0, 1)], x_ref.at[pl.ds(0, 1)]),
        ))
    ]
    load_rates, load_residues, load_spans, load_edge, load_taps, load_kv, load_q = loads
    for load in loads:
        load.start()

    barrier = pltpu.get_barrier_semaphore()
    for step in steps:
        @pl.when(z >= step)
        def _():
            pl.semaphore_signal(barrier, inc=1, device_id={"seq": z - step}, device_id_type=MESH)
    for axis, me, count in (("grp", g, grp), ("sub", s, sub)):
        for step in range(1, count):
            pl.semaphore_signal(
                barrier, inc=1, device_id={axis: lax.rem(me + step, count)}, device_id_type=MESH
            )
    load_weight = pltpu.make_async_copy(weight_hbm, weight, weight_sem)
    load_weight.start()

    if pitch != rows:
        for buffer in (gates, mode_rows):
            buffer[...] = jnp.zeros_like(buffer)
    incoming[...] = jnp.zeros_like(incoming)
    for buffer in (wide_k, wide_v):
        buffer[:, pl.ds(0, HEAD), :] = jnp.zeros((rows, HEAD, LANES), F32)

    load_spans.wait()
    starts, start = [], jnp.int32(0)
    for i in range(spans_ref.shape[0]):
        starts.append(start)
        start = start + spans_ref[i]
    latest = jnp.int32(0)
    for first in starts:
        latest = jnp.where(first < offset + tokens, first, latest)
    position = offset - HEAD + lax.broadcasted_iota(jnp.int32, (tokens + HEAD, LANES), 0)
    here = position == starts[0]
    for first in starts[1:]:
        here = here | (position == first)
    keep1[...] = jnp.where(here, 0.0, 1.0)
    keep2[...] = keep1[pl.ds(HEAD, tokens), :] * keep1[pl.ds(HEAD - 1, tokens), :]

    load_rates.wait()
    load_residues.wait()
    rates = rates_ref[...]
    token = lax.broadcasted_iota(jnp.int32, (modes, tokens), 1)
    ahead = (token - (tokens - 1)).astype(F32)
    live = jnp.where((offset + token >= latest) & (token >= 2), 1.0, 0.0)
    for c in range(rows):
        for i in range(per_row):
            rate = jnp.broadcast_to(rates[:, c * per_row + i : c * per_row + i + 1], (modes, tokens))
            power = jnp.exp(rate * ahead) * live
            high = power.astype(BF16).astype(F32)
            wide_at = pl.ds(i * modes, modes)
            powers[c, wide_at, :] = high
            powers[c, pl.ds((per_row + i) * modes, modes), :] = power - high

    spread = (
        lax.broadcasted_iota(jnp.int32, (groups, channels), 1) // group_size
        == lax.broadcasted_iota(jnp.int32, (groups, channels), 0)
    ).astype(F32)
    drop = tanh(rates) * (1.0 + jnp.exp(-2.0 * rates))
    for first, values in ((0, rates), (modes, residues_ref[...] * jnp.sqrt(drop))):
        wide = jnp.dot(values, spread, precision=lax.Precision.HIGHEST, preferred_element_type=F32)
        if first == 0:
            wide_rates[...] = wide
            for t in range(2):
                first_live = jnp.where(offset + t >= latest, 1.0, 0.0)
                first_powers[t] = jnp.exp(wide * (-float(tokens - 1 - t))) * first_live
        for c in range(rows):
            mode_rows[pl.ds(first * pitch + c, modes, stride=pitch), :] = wide[
                :, c * LANES : (c + 1) * LANES
            ]

    load_edge.wait()
    for j in range(3):
        for c in range(rows):
            lanes = slice(c * LANES, (c + 1) * LANES)
            halo_rows[pl.ds(2 * j * pitch + c, 2, stride=pitch), :] = edge_ref[j, :, lanes].astype(F32)[EDGE - 2 :]
    halo_out[...] = halo_rows[...].astype(BF16)

    load_taps.wait()

    def lanes_of(c):
        if isinstance(c, int):
            return slice(c * LANES, (c + 1) * LANES)
        return pl.ds(pl.multiple_of(c * LANES, LANES), LANES)

    def filtered(j, buffer, c, lower, count):
        tap = [taps_ref[k, pl.ds(j, 1), lanes_of(c)] for k in range(3)]
        now, last, older = (buffer[c, pl.ds(HEAD + lower - k, count), :] for k in range(3))
        m1, m2 = keep1[pl.ds(HEAD + lower, count), :], keep2[pl.ds(lower, count), :]
        return tap[0] * now + tap[1] * last * m1 + tap[2] * older * m2

    def gate(c, lower, count):
        value = (filtered(1, wide_k, c, lower, count) * filtered(2, wide_v, c, lower, count)).astype(BF16)
        gathered[0, pl.ds(lower, count), lanes_of(c)] = value
        gates[pl.ds(lower * pitch + c, count, stride=pitch), :] = value.astype(F32)

    load_kv.wait()
    block = 64

    def gate_rows(c, carry):
        for j, buffer in ((1, wide_k), (2, wide_v)):
            buffer[c, pl.ds(HEAD, tokens), :] = x_ref[j, :, lanes_of(c)].astype(F32)
        lower = 0
        while lower < tokens:
            count = min(block, tokens - lower)
            gate(c, lower, count)
            lower += count
        return carry

    lax.fori_loop(0, rows, gate_rows, 0)

    pl.semaphore_wait(barrier, jnp.minimum(reach_steps, seq - 1 - z) + grp + sub - 2)

    send_halo = pltpu.make_async_remote_copy(
        src_ref=halo_out, dst_ref=halo_in, send_sem=halo_send, recv_sem=halo_recv,
        device_id={"seq": lax.rem(z + 1, seq)}, device_id_type=MESH,
    )

    @pl.when(z < seq - 1)
    def _():
        send_halo.start()

    lane_group = lax.broadcasted_iota(jnp.int32, (modes, LANES), 1) // group_size
    for c in range(rows):
        lanes = slice(c * LANES, (c + 1) * LANES)
        sums = jnp.dot(powers[c].astype(BF16), gathered[0, :, lanes], preferred_element_type=F32)
        sums = sums[: per_row * modes] + sums[per_row * modes :]
        state = sums[:modes]
        for i in range(1, per_row):
            state = jnp.where(lane_group == i, sums[i * modes : (i + 1) * modes], state)
        partial[:, lanes] = state

    @pl.when(z == 0)
    def _():
        halo_in[...] = jnp.zeros_like(halo_in)

    @pl.when(z > 0)
    def _():
        send_halo.wait_recv()

    halo_rows[...] = halo_in[...].astype(F32)
    for j, buffer in enumerate((wide_q, wide_k, wide_v)):
        for c in range(rows):
            buffer[c, pl.ds(HEAD - 2, 2), :] = halo_rows[pl.ds(2 * j * pitch + c, 2, stride=pitch), :]
    for c in range(rows):
        lanes = slice(c * LANES, (c + 1) * LANES)
        value = filtered(1, wide_k, c, 0, HEAD) * filtered(2, wide_v, c, 0, HEAD)
        value = value.astype(BF16).astype(F32)
        gates[pl.ds(c, HEAD, stride=pitch), :] = value
        state = partial[:, lanes] + first_powers[0, :, lanes] * value[0:1] + first_powers[1, :, lanes] * value[1:2]
        half = c * 2 // rows
        state_out[pl.ds(half * modes, modes), slice((c - half * rows // 2) * LANES, (c - half * rows // 2 + 1) * LANES)] = state

    state_sent[...] = state_out[...].astype(BF16)
    state_copies = []
    for step in steps:
        copy = pltpu.make_async_remote_copy(
            src_ref=state_sent, dst_ref=state_in.at[step - 1],
            send_sem=state_send.at[step - 1], recv_sem=state_recv.at[step - 1],
            device_id={"seq": lax.rem(z + step, seq)}, device_id_type=MESH,
        )
        state_copies.append(copy)
    for step in reversed(steps):
        pl.when(z + step < seq)(state_copies[step - 1].start)

    def tile(ref, index):
        return ref[pl.ds(pl.multiple_of(index * pitch, pitch), pitch), :]

    decay = [jnp.exp(-tile(mode_rows, n)) for n in range(modes)]
    gain = [tile(mode_rows, modes + n) for n in range(modes)]
    load_q.wait()

    for step in steps:
        reach = (step - 1) * tokens
        open_ = jnp.float32(1.0)
        for first in starts:
            inside = (first >= offset - reach) & (first <= offset - 1)
            open_ = jnp.where(inside, 0.0, open_)

        @pl.when(z >= step)
        def _():
            state_copies[step - 1].wait_recv()
            came = state_in[step - 1].astype(F32)
            for c in range(rows):
                lanes = slice(c * LANES, (c + 1) * LANES)
                half = c * 2 // rows
                left = (c - half * rows // 2) * LANES
                part = came[half * modes : (half + 1) * modes, left : left + LANES] * open_
                if reach:
                    part = part * jnp.exp(wide_rates[:, lanes] * (-float(reach)))
                at = pl.ds(c, modes, stride=pitch)
                incoming[at, :] = incoming[at, :] + part

    own = g * sub + s
    carried = [tile(incoming, n) for n in range(modes)]
    unroll = 8

    def combine(parts):
        while len(parts) > 1:
            parts = [sum(parts[i + 1 : i + 2], parts[i]) for i in range(0, len(parts), 2)]
        return parts[0]

    def advance(block, state):
        for u in range(unroll):
            t = block * unroll + u
            gated, m1 = tile(gates, t), keep1[pl.ds(HEAD + t, 1), :]
            state = [decay[n] * (state[n] * m1) + gated for n in range(modes)]
            rows_out[pl.ds(pl.multiple_of(t * pitch, pitch), pitch), :] = combine(
                [gain[n] * state[n] for n in range(modes)]
            )
        return state

    def send(slot, c, axis, me, count, step, send_sem, recv_sem):
        lower, size = pieces[c]
        piece = gathered.at[1 + slot, pl.ds(lower, size), :]
        return pltpu.make_async_remote_copy(
            src_ref=piece, dst_ref=piece, send_sem=send_sem, recv_sem=recv_sem,
            device_id={axis: lax.rem(me + step, count)}, device_id_type=MESH,
        )

    def over_sub(slot, c):
        return send(slot, c, "sub", s, sub, 1, sub_send.at[c], sub_recv.at[c])

    def over_grp(slot, c, step):
        return send(slot, c, "grp", g, grp, step, grp_send.at[step - 1, c], grp_recv.at[step - 1, c])

    def onward(slot, c, step):
        return send(slot, c, "sub", s, sub, 1, fwd_send.at[step - 1, c], fwd_recv.at[step - 1, c])

    for c, (lower, size) in enumerate(pieces):
        carried = lax.fori_loop(lower // unroll, (lower + size) // unroll, advance, carried)

        def mix(r, carry):
            wide_q[r, pl.ds(HEAD + lower, size), :] = x_ref[0, pl.ds(lower, size), lanes_of(r)].astype(F32)
            long_out = rows_out[pl.ds(lower * pitch + r, size, stride=pitch), :]
            gathered[1 + own, pl.ds(lower, size), lanes_of(r)] = (
                filtered(0, wide_q, r, lower, size) * long_out
            ).astype(BF16)
            return carry

        lax.fori_loop(0, rows, mix, 0)
        for step in range(1, grp):
            if c < held:
                over_grp(own, c, step).start()
            else:
                pl.when(s == 0)(over_grp(own, c, step).start)
        over_sub(own, c).start()

    def product(slot, lower, count):
        depth = pl.ds(pl.multiple_of(slot * channels, channels), channels)
        return jnp.dot(
            gathered[1 + slot, pl.ds(lower, count), :], weight[depth, :], preferred_element_type=F32
        )

    load_weight.wait()
    total[...] = product(own, 0, tokens)
    other = g * sub + 1 - s
    for c in range(len(pieces)):
        over_sub(other, c).wait_recv()
    total[...] += product(other, 0, tokens)

    def extent(members):
        return pieces[members[0]][0], sum(pieces[c][1] for c in members)

    def direct(members):
        lower, count = extent(members)
        at = pl.ds(lower, count)
        for step in range(1, grp):
            slot = lax.rem(g + grp - step, grp) * sub + s
            for c in members:
                over_grp(slot, c, step).wait_recv()
                onward(slot, c, step).start()
            total[at, :] += product(slot, lower, count)

    def forwarded(members):
        lower, count = extent(members)
        at = pl.ds(lower, count)
        for step in range(1, grp):
            slot = lax.rem(g + grp - step, grp) * sub + 1 - s
            for c in members:
                onward(slot, c, step).wait_recv()
                if step == 1 and c == trigger:
                    @pl.when(s == 1)
                    def _():
                        for way in range(1, grp):
                            over_grp(own, held, way).start()
            value = total[at, :] + product(slot, lower, count)
            if step < grp - 1:
                total[at, :] = value
            else:
                out_ref[at, :] = value.astype(out_ref.dtype)

    for members in groupings:
        direct(members)
        forwarded(members)

    for step in range(1, grp):
        for c in range(len(pieces)):
            over_grp(own, c, step).wait_send()
            onward(own, c, step).wait_send()
    for c in range(len(pieces)):
        over_sub(own, c).wait_send()
    pl.when(z < seq - 1)(send_halo.wait_send)
    for step in steps:
        pl.when(z + step < seq)(state_copies[step - 1].wait_send)


def shards(sizes, projected, short_filter, span_lengths, mode_rates, mode_residues, out_weight):
    seq, grp, sub = sizes
    tokens, _, channels = projected.shape
    modes, groups = mode_rates.shape
    rows = channels // LANES
    pitch = -(-rows // 8) * 8
    reach_steps = min(seq - 1, (seq * tokens // 2 - 1 + tokens - 1) // tokens)
    sizes_of = (16, 48, 32, 32, 64, 64)
    pieces = tuple((sum(sizes_of[:i]), size) for i, size in enumerate(sizes_of))
    count = len(pieces)
    groupings, trigger = ((0, 1, 2, 3), (4,), (5,)), 3
    per_row = LANES * groups // channels
    streams = projected.transpose(1, 0, 2)
    vmem = pl.BlockSpec(memory_space=pltpu.VMEM)
    hbm = pl.BlockSpec(memory_space=pl.ANY)
    dma = pltpu.SemaphoreType.DMA
    row_tile = pltpu.VMEM((tokens * pitch, LANES), F32)
    stream = pltpu.VMEM((rows, tokens + HEAD, LANES), F32)
    state, packed = (modes, channels), (2 * modes, channels // 2)
    return pl.pallas_call(
        functools.partial(kernel, (seq, grp, sub, reach_steps, pieces, groupings, trigger)),
        out_shape=pltpu.VMEM((tokens, out_weight.shape[1]), BF16),
        in_specs=[hbm] * 6,
        out_specs=vmem,
        scratch_shapes=[
            pltpu.SMEM(span_lengths.shape, jnp.int32),
            pltpu.VMEM(streams.shape, BF16),
            pltpu.VMEM((3, EDGE, channels), BF16),
            pltpu.VMEM(short_filter.shape, F32),
            pltpu.VMEM(mode_rates.shape, F32),
            pltpu.VMEM(mode_residues.shape, F32),
            pltpu.VMEM(out_weight.shape, BF16),
            stream, stream, stream,
            pltpu.VMEM((tokens + HEAD, LANES), F32),
            pltpu.VMEM((tokens, LANES), F32),
            pltpu.VMEM((rows, 2 * per_row * modes, tokens), F32),
            pltpu.VMEM((2 * modes * pitch, LANES), F32),
            pltpu.VMEM(state, F32),
            pltpu.VMEM((2,) + state, F32),
            pltpu.VMEM(state, F32),
            row_tile, row_tile,
            pltpu.VMEM((6 * pitch, LANES), F32),
            pltpu.VMEM((6 * pitch, LANES), BF16),
            pltpu.VMEM((6 * pitch, LANES), BF16),
            pltpu.VMEM(packed, F32),
            pltpu.VMEM(packed, BF16),
            pltpu.VMEM((reach_steps,) + packed, BF16),
            pltpu.VMEM((modes * pitch, LANES), F32),
            pltpu.VMEM((1 + grp * sub, tokens, channels), BF16),
            pltpu.VMEM((tokens, out_weight.shape[1]), F32),
            dma((7,)), dma, dma, dma,
            dma((reach_steps,)), dma((reach_steps,)),
            dma((count,)), dma((count,)),
            dma((grp - 1, count)), dma((grp - 1, count)),
            dma((grp - 1, count)), dma((grp - 1, count)),
        ],
        compiler_params=pltpu.CompilerParams(collective_id=0, has_side_effects=True),
    )(span_lengths, streams, short_filter, mode_rates, mode_residues, out_weight)


def solution(mesh):
    sizes = (mesh.shape["seq"], mesh.shape["grp"], mesh.shape["sub"])
    return jax.shard_map(
        functools.partial(shards, sizes),
        mesh=mesh,
        in_specs=(
            P(("parts", "seq"), None, ("grp", "sub")),
            P(None, None, ("grp", "sub")),
            P("parts"),
            P(None, ("grp", "sub")),
            P(None, ("grp", "sub")),
            P(None, ("grp", "sub")),
        ),
        out_specs=P(("parts", "seq"), ("grp", "sub")),
        check_vma=False,
    )
```

```python
import functools

import jax
import jax.numpy as jnp
from jax import lax
from jax.experimental import pallas as pl
from jax.experimental.pallas import tpu as pltpu
from jax.sharding import PartitionSpec as P

MESH = pl.DeviceIdType.MESH
LANES = 128
HEAD = 8
EDGE = 16
F32, BF16 = jnp.float32, jnp.bfloat16


def tanh(x):
    x = jnp.clip(x, -7.90531110763549805, 7.90531110763549805)
    square = x * x
    top = jnp.full_like(x, -2.76076847742355e-16)
    for c in (
        2.00018790482477e-13, -8.60467152213735e-11, 5.12229709037114e-08,
        1.48572235717979e-05, 6.37261928875436e-04, 4.89352455891786e-03,
    ):
        top = top * square + c
    bottom = jnp.full_like(x, 1.19825839466702e-06)
    for c in (1.18534705686654e-04, 2.26843463243900e-03, 4.89352518554385e-03):
        bottom = bottom * square + c
    return jnp.where(jnp.abs(x) < 0.0004, x, x * top / bottom)


def kernel(
    sizes, spans_hbm, x_hbm, taps_hbm, rates_hbm, residues_hbm, weight_hbm, out_ref,
    spans_ref, x_ref, edge_ref, taps_ref, rates_ref, residues_ref, weight,
    wide_q, wide_k, wide_v, keep1, keep2, powers, mode_rows, wide_rates, first_powers, partial,
    gates, rows_out, halo_rows, halo_out, halo_in, state_out, state_sent, state_in, incoming,
    gathered, total,
    load_sems, weight_sem, ready, halo_send, halo_recv, state_send, state_recv,
    sub_send, sub_recv, grp_send, grp_recv, fwd_send, fwd_recv,
):
    seq, grp, sub, reach_steps, pieces, groupings, trigger = sizes
    _, tokens, channels = x_ref.shape
    modes, groups = rates_ref.shape
    held = range(len(pieces) - 2, len(pieces))
    rows = channels // LANES
    pitch = gates.shape[0] // tokens
    group_size = channels // groups
    per_row = LANES // group_size
    steps = range(1, reach_steps + 1)
    z, g, s = lax.axis_index("seq"), lax.axis_index("grp"), lax.axis_index("sub")
    offset = z * tokens

    barrier = pltpu.get_barrier_semaphore()
    @pl.when(z > 0)
    def _():
        pl.semaphore_signal(barrier, inc=1, device_id={"seq": z - 1}, device_id_type=MESH)

    @pl.when(z < seq - 1)
    def _():
        pl.semaphore_signal(barrier, inc=1, device_id={"seq": z + 1}, device_id_type=MESH)

    for axis, me, count in (("grp", g, grp), ("sub", s, sub)):
        for step in range(1, count):
            pl.semaphore_signal(
                barrier, inc=1, device_id={axis: lax.rem(me + step, count)}, device_id_type=MESH
            )
    loads = [
        pltpu.make_async_copy(source, target, load_sems.at[i])
        for i, (source, target) in enumerate((
            (rates_hbm, rates_ref), (residues_hbm, residues_ref), (spans_hbm, spans_ref),
            (x_hbm.at[:, pl.ds(tokens - EDGE, EDGE), :], edge_ref), (taps_hbm, taps_ref),
            (x_hbm.at[pl.ds(1, 2)], x_ref.at[pl.ds(1, 2)]), (x_hbm.at[pl.ds(0, 1)], x_ref.at[pl.ds(0, 1)]),
        ))
    ]
    load_rates, load_residues, load_spans, load_edge, load_taps, load_kv, load_q = loads
    for load in loads:
        load.start()

    load_weight = pltpu.make_async_copy(weight_hbm, weight, weight_sem)
    load_weight.start()

    if pitch != rows:
        for buffer in (gates, mode_rows):
            buffer[...] = jnp.zeros_like(buffer)
    incoming[...] = jnp.zeros_like(incoming)
    for buffer in (wide_k, wide_v):
        buffer[:, pl.ds(0, HEAD), :] = jnp.zeros((rows, HEAD, LANES), F32)

    load_spans.wait()
    starts, start = [], jnp.int32(0)
    for i in range(spans_ref.shape[0]):
        starts.append(start)
        start = start + spans_ref[i]
    latest = jnp.int32(0)
    for first in starts:
        latest = jnp.where(first < offset + tokens, first, latest)
    position = offset - HEAD + lax.broadcasted_iota(jnp.int32, (tokens + HEAD, LANES), 0)
    here = position == starts[0]
    for first in starts[1:]:
        here = here | (position == first)
    keep1[...] = jnp.where(here, 0.0, 1.0)
    keep2[...] = keep1[pl.ds(HEAD, tokens), :] * keep1[pl.ds(HEAD - 1, tokens), :]

    load_rates.wait()
    load_residues.wait()
    rates = rates_ref[...]
    token = lax.broadcasted_iota(jnp.int32, (modes, tokens), 1)
    ahead = (token - (tokens - 1)).astype(F32)
    live = jnp.where((offset + token >= latest) & (token >= 2), 1.0, 0.0)
    for c in range(rows):
        for i in range(per_row):
            rate = jnp.broadcast_to(rates[:, c * per_row + i : c * per_row + i + 1], (modes, tokens))
            power = jnp.exp(rate * ahead) * live
            high = power.astype(BF16).astype(F32)
            wide_at = pl.ds(i * modes, modes)
            powers[c, wide_at, :] = high
            powers[c, pl.ds((per_row + i) * modes, modes), :] = power - high

    spread = (
        lax.broadcasted_iota(jnp.int32, (groups, channels), 1) // group_size
        == lax.broadcasted_iota(jnp.int32, (groups, channels), 0)
    ).astype(F32)
    drop = tanh(rates) * (1.0 + jnp.exp(-2.0 * rates))
    for first, values in ((0, rates), (modes, residues_ref[...] * jnp.sqrt(drop))):
        wide = jnp.dot(values, spread, precision=lax.Precision.HIGHEST, preferred_element_type=F32)
        if first == 0:
            wide_rates[...] = wide
            for t in range(2):
                first_live = jnp.where(offset + t >= latest, 1.0, 0.0)
                first_powers[t] = jnp.exp(wide * (-float(tokens - 1 - t))) * first_live
        for c in range(rows):
            mode_rows[pl.ds(first * pitch + c, modes, stride=pitch), :] = wide[
                :, c * LANES : (c + 1) * LANES
            ]

    load_edge.wait()
    for j in range(3):
        for c in range(rows):
            lanes = slice(c * LANES, (c + 1) * LANES)
            halo_rows[pl.ds(2 * j * pitch + c, 2, stride=pitch), :] = edge_ref[j, :, lanes].astype(F32)[EDGE - 2 :]
    halo_out[...] = halo_rows[...].astype(BF16)

    load_taps.wait()

    def lanes_of(c):
        if isinstance(c, int):
            return slice(c * LANES, (c + 1) * LANES)
        return pl.ds(pl.multiple_of(c * LANES, LANES), LANES)

    def filtered(j, buffer, c, lower, count):
        tap = [taps_ref[k, pl.ds(j, 1), lanes_of(c)] for k in range(3)]
        now, last, older = (buffer[c, pl.ds(HEAD + lower - k, count), :] for k in range(3))
        m1, m2 = keep1[pl.ds(HEAD + lower, count), :], keep2[pl.ds(lower, count), :]
        return tap[0] * now + tap[1] * last * m1 + tap[2] * older * m2

    def gate(c, lower, count):
        value = (filtered(1, wide_k, c, lower, count) * filtered(2, wide_v, c, lower, count)).astype(BF16)
        gathered[0, pl.ds(lower, count), lanes_of(c)] = value
        gates[pl.ds(lower * pitch + c, count, stride=pitch), :] = value.astype(F32)

    load_kv.wait()
    block = 64

    def gate_rows(c, carry):
        for j, buffer in ((1, wide_k), (2, wide_v)):
            buffer[c, pl.ds(HEAD, tokens), :] = x_ref[j, :, lanes_of(c)].astype(F32)
        lower = 0
        while lower < tokens:
            count = min(block, tokens - lower)
            gate(c, lower, count)
            lower += count
        return carry

    lax.fori_loop(0, rows, gate_rows, 0)

    pl.semaphore_wait(barrier, jnp.minimum(seq - 1 - z, 1) + jnp.minimum(z, 1) + grp + sub - 2)

    send_halo = pltpu.make_async_remote_copy(
        src_ref=halo_out, dst_ref=halo_in, send_sem=halo_send, recv_sem=halo_recv,
        device_id={"seq": lax.rem(z + 1, seq)}, device_id_type=MESH,
    )

    @pl.when(z < seq - 1)
    def _():
        send_halo.start()

    def tell(step):
        @pl.when((z > 0) & (z + step - 1 < seq))
        def _():
            pl.semaphore_signal(
                ready.at[step - 1], inc=1, device_id={"seq": z - 1}, device_id_type=MESH
            )

    if reach_steps > 1:
        tell(2)

    lane_group = lax.broadcasted_iota(jnp.int32, (modes, LANES), 1) // group_size
    for c in range(rows):
        lanes = slice(c * LANES, (c + 1) * LANES)
        sums = jnp.dot(powers[c].astype(BF16), gathered[0, :, lanes], preferred_element_type=F32)
        sums = sums[: per_row * modes] + sums[per_row * modes :]
        state = sums[:modes]
        for i in range(1, per_row):
            state = jnp.where(lane_group == i, sums[i * modes : (i + 1) * modes], state)
        partial[:, lanes] = state

    @pl.when(z == 0)
    def _():
        halo_in[...] = jnp.zeros_like(halo_in)

    @pl.when(z > 0)
    def _():
        send_halo.wait_recv()

    halo_rows[...] = halo_in[...].astype(F32)
    for j, buffer in enumerate((wide_q, wide_k, wide_v)):
        for c in range(rows):
            buffer[c, pl.ds(HEAD - 2, 2), :] = halo_rows[pl.ds(2 * j * pitch + c, 2, stride=pitch), :]
    for c in range(rows):
        lanes = slice(c * LANES, (c + 1) * LANES)
        value = filtered(1, wide_k, c, 0, HEAD) * filtered(2, wide_v, c, 0, HEAD)
        value = value.astype(BF16).astype(F32)
        gates[pl.ds(c, HEAD, stride=pitch), :] = value
        state = partial[:, lanes] + first_powers[0, :, lanes] * value[0:1] + first_powers[1, :, lanes] * value[1:2]
        half = c * 2 // rows
        state_out[pl.ds(half * modes, modes), slice((c - half * rows // 2) * LANES, (c - half * rows // 2 + 1) * LANES)] = state

    state_sent[...] = state_out[...].astype(BF16)
    state_copies = []
    for step in steps:
        copy = pltpu.make_async_remote_copy(
            src_ref=state_sent, dst_ref=state_in.at[step - 1],
            send_sem=state_send.at[step - 1], recv_sem=state_recv.at[step - 1],
            device_id={"seq": lax.rem(z + step, seq)}, device_id_type=MESH,
        )
        state_copies.append(copy)
    for step in steps:
        @pl.when(z + step < seq)
        def _():
            if step > 1:
                pl.semaphore_wait(ready.at[step - 1], 1)
            state_copies[step - 1].start()

        if 1 < step < reach_steps:
            tell(step + 1)

    def tile(ref, index):
        return ref[pl.ds(pl.multiple_of(index * pitch, pitch), pitch), :]

    decay = [jnp.exp(-tile(mode_rows, n)) for n in range(modes)]
    gain = [tile(mode_rows, modes + n) for n in range(modes)]
    load_q.wait()

    for step in steps:
        reach = (step - 1) * tokens
        open_ = jnp.float32(1.0)
        for first in starts:
            inside = (first >= offset - reach) & (first <= offset - 1)
            open_ = jnp.where(inside, 0.0, open_)

        @pl.when(z >= step)
        def _():
            state_copies[step - 1].wait_recv()
            came = state_in[step - 1].astype(F32)
            for c in range(rows):
                lanes = slice(c * LANES, (c + 1) * LANES)
                half = c * 2 // rows
                left = (c - half * rows // 2) * LANES
                part = came[half * modes : (half + 1) * modes, left : left + LANES] * open_
                if reach:
                    part = part * jnp.exp(wide_rates[:, lanes] * (-float(reach)))
                at = pl.ds(c, modes, stride=pitch)
                incoming[at, :] = incoming[at, :] + part

    own = g * sub + s
    carried = [tile(incoming, n) for n in range(modes)]
    unroll = 8

    def combine(parts):
        while len(parts) > 1:
            parts = [sum(parts[i + 1 : i + 2], parts[i]) for i in range(0, len(parts), 2)]
        return parts[0]

    def advance(block, state):
        for u in range(unroll):
            t = block * unroll + u
            gated, m1 = tile(gates, t), keep1[pl.ds(HEAD + t, 1), :]
            state = [decay[n] * (state[n] * m1) + gated for n in range(modes)]
            rows_out[pl.ds(pl.multiple_of(t * pitch, pitch), pitch), :] = combine(
                [gain[n] * state[n] for n in range(modes)]
            )
        return state

    def send(slot, c, axis, me, count, step, send_sem, recv_sem):
        lower, size, left, width = pieces[c]
        piece = gathered.at[1 + slot, pl.ds(lower, size), pl.ds(left, width)]
        return pltpu.make_async_remote_copy(
            src_ref=piece, dst_ref=piece, send_sem=send_sem, recv_sem=recv_sem,
            device_id={axis: lax.rem(me + step, count)}, device_id_type=MESH,
        )

    def over_sub(slot, c):
        return send(slot, c, "sub", s, sub, 1, sub_send.at[c], sub_recv.at[c])

    def over_grp(slot, c, step):
        return send(slot, c, "grp", g, grp, step, grp_send.at[step - 1, c], grp_recv.at[step - 1, c])

    def onward(slot, c, step):
        return send(slot, c, "sub", s, sub, 1, fwd_send.at[step - 1, c], fwd_recv.at[step - 1, c])

    for c, (lower, size, left, width) in enumerate(pieces):
        carried = carried if left else lax.fori_loop(lower // unroll, (lower + size) // unroll, advance, carried)

        def mix(r, carry):
            wide_q[r, pl.ds(HEAD + lower, size), :] = x_ref[0, pl.ds(lower, size), lanes_of(r)].astype(F32)
            long_out = rows_out[pl.ds(lower * pitch + r, size, stride=pitch), :]
            gathered[1 + own, pl.ds(lower, size), lanes_of(r)] = (
                filtered(0, wide_q, r, lower, size) * long_out
            ).astype(BF16)
            return carry

        if c == 0:
            for r in range(rows):
                mix(r, 0)
        else:
            lax.fori_loop(left // LANES, (left + width) // LANES, mix, 0)
        for step in range(1, grp):
            if c not in held:
                over_grp(own, c, step).start()
            else:
                pl.when(s == 0)(over_grp(own, c, step).start)
        over_sub(own, c).start()

    def product(slot, lower, count, left=0, width=channels):
        depth = pl.ds(pl.multiple_of(slot * channels + left, width), width)
        return jnp.dot(
            gathered[1 + slot, pl.ds(lower, count), pl.ds(left, width)], weight[depth, :],
            preferred_element_type=F32,
        )

    load_weight.wait()
    total[...] = product(own, 0, tokens)
    other = g * sub + 1 - s
    for c in range(len(pieces)):
        over_sub(other, c).wait_recv()
    total[...] += product(other, 0, tokens)

    def extent(members):
        return pieces[members[0]][0], sum(pieces[c][1] for c in members), *pieces[members[0]][2:]

    def direct(members):
        lower, count, left, width = extent(members)
        at = pl.ds(lower, count)
        for step in range(1, grp):
            slot = lax.rem(g + grp - step, grp) * sub + s
            for c in members:
                over_grp(slot, c, step).wait_recv()
                onward(slot, c, step).start()
            total[at, :] += product(slot, lower, count, left, width)

    def forwarded(members):
        lower, count, left, width = extent(members)
        at = pl.ds(lower, count)
        for step in range(1, grp):
            slot = lax.rem(g + grp - step, grp) * sub + 1 - s
            for c in members:
                onward(slot, c, step).wait_recv()
                if step == 1 and c == trigger:
                    @pl.when(s == 1)
                    def _():
                        for late in held:
                            for way in range(1, grp):
                                over_grp(own, late, way).start()
            value = total[at, :] + product(slot, lower, count, left, width)
            if step < grp - 1 or left + width < channels:
                total[at, :] = value
            else:
                out_ref[at, :] = value.astype(out_ref.dtype)

    for members in groupings[:-2]:
        direct(members)
        forwarded(members)
    for members in groupings[-2:]:
        direct(members)
    for members in groupings[-2:]:
        forwarded(members)

    for step in range(1, grp):
        for c in range(len(pieces)):
            over_grp(own, c, step).wait_send()
            onward(own, c, step).wait_send()
    for c in range(len(pieces)):
        over_sub(own, c).wait_send()
    pl.when(z < seq - 1)(send_halo.wait_send)
    for step in steps:
        pl.when(z + step < seq)(state_copies[step - 1].wait_send)


def shards(sizes, projected, short_filter, span_lengths, mode_rates, mode_residues, out_weight):
    seq, grp, sub = sizes
    tokens, _, channels = projected.shape
    modes, groups = mode_rates.shape
    rows = channels // LANES
    pitch = -(-rows // 8) * 8
    reach_steps = min(seq - 1, (seq * tokens // 2 - 1 + tokens - 1) // tokens)
    sizes_of = (16, 48, 32, 32, 64, 64)
    pieces = [(sum(sizes_of[:i]), size, 0, channels) for i, size in enumerate(sizes_of)]
    lower, size, left, width = pieces.pop()
    half = width // 2
    pieces = (*pieces, (lower, size, 0, half), (lower, size, half, half))
    count = len(pieces)
    groupings, trigger = ((0, 1, 2, 3), (4,), (5,), (6,)), 3
    per_row = LANES * groups // channels
    streams = projected.transpose(1, 0, 2)
    vmem = pl.BlockSpec(memory_space=pltpu.VMEM)
    hbm = pl.BlockSpec(memory_space=pl.ANY)
    dma = pltpu.SemaphoreType.DMA
    row_tile = pltpu.VMEM((tokens * pitch, LANES), F32)
    stream = pltpu.VMEM((rows, tokens + HEAD, LANES), F32)
    state, packed = (modes, channels), (2 * modes, channels // 2)
    return pl.pallas_call(
        functools.partial(kernel, (seq, grp, sub, reach_steps, pieces, groupings, trigger)),
        out_shape=pltpu.VMEM((tokens, out_weight.shape[1]), BF16),
        in_specs=[hbm] * 6,
        out_specs=vmem,
        scratch_shapes=[
            pltpu.SMEM(span_lengths.shape, jnp.int32),
            pltpu.VMEM(streams.shape, BF16),
            pltpu.VMEM((3, EDGE, channels), BF16),
            pltpu.VMEM(short_filter.shape, F32),
            pltpu.VMEM(mode_rates.shape, F32),
            pltpu.VMEM(mode_residues.shape, F32),
            pltpu.VMEM(out_weight.shape, BF16),
            stream, stream, stream,
            pltpu.VMEM((tokens + HEAD, LANES), F32),
            pltpu.VMEM((tokens, LANES), F32),
            pltpu.VMEM((rows, 2 * per_row * modes, tokens), F32),
            pltpu.VMEM((2 * modes * pitch, LANES), F32),
            pltpu.VMEM(state, F32),
            pltpu.VMEM((2,) + state, F32),
            pltpu.VMEM(state, F32),
            row_tile, row_tile,
            pltpu.VMEM((6 * pitch, LANES), F32),
            pltpu.VMEM((6 * pitch, LANES), BF16),
            pltpu.VMEM((6 * pitch, LANES), BF16),
            pltpu.VMEM(packed, F32),
            pltpu.VMEM(packed, BF16),
            pltpu.VMEM((reach_steps,) + packed, BF16),
            pltpu.VMEM((modes * pitch, LANES), F32),
            pltpu.VMEM((1 + grp * sub, tokens, channels), BF16),
            pltpu.VMEM((tokens, out_weight.shape[1]), F32),
            dma((7,)), dma, pltpu.SemaphoreType.REGULAR((reach_steps,)), dma, dma,
            dma((reach_steps,)), dma((reach_steps,)),
            dma((count,)), dma((count,)),
            dma((grp - 1, count)), dma((grp - 1, count)),
            dma((grp - 1, count)), dma((grp - 1, count)),
        ],
        compiler_params=pltpu.CompilerParams(collective_id=0, has_side_effects=True),
    )(span_lengths, streams, short_filter, mode_rates, mode_residues, out_weight)


def solution(mesh):
    sizes = (mesh.shape["seq"], mesh.shape["grp"], mesh.shape["sub"])
    return jax.shard_map(
        functools.partial(shards, sizes),
        mesh=mesh,
        in_specs=(
            P(("parts", "seq"), None, ("grp", "sub")),
            P(None, None, ("grp", "sub")),
            P("parts"),
            P(None, ("grp", "sub")),
            P(None, ("grp", "sub")),
            P(None, ("grp", "sub")),
        ),
        out_specs=P(("parts", "seq"), ("grp", "sub")),
        check_vma=False,
    )
```

```python
import functools

import jax
import jax.numpy as jnp
from jax import lax
from jax.experimental import pallas as pl
from jax.experimental.pallas import tpu as pltpu
from jax.sharding import PartitionSpec as P

MESH = pl.DeviceIdType.MESH
LANES = 128
HEAD = 8
EDGE = 16
F32, BF16 = jnp.float32, jnp.bfloat16


def tanh(x):
    x = jnp.clip(x, -7.90531110763549805, 7.90531110763549805)
    square = x * x
    top = jnp.full_like(x, -2.76076847742355e-16)
    for c in (
        2.00018790482477e-13, -8.60467152213735e-11, 5.12229709037114e-08,
        1.48572235717979e-05, 6.37261928875436e-04, 4.89352455891786e-03,
    ):
        top = top * square + c
    bottom = jnp.full_like(x, 1.19825839466702e-06)
    for c in (1.18534705686654e-04, 2.26843463243900e-03, 4.89352518554385e-03):
        bottom = bottom * square + c
    return jnp.where(jnp.abs(x) < 0.0004, x, x * top / bottom)


def kernel(
    sizes, spans_hbm, x_hbm, taps_hbm, rates_hbm, residues_hbm, weight_hbm, out_ref,
    spans_ref, x_ref, edge_ref, taps_ref, rates_ref, residues_ref, weight,
    wide_q, wide_k, wide_v, keep1, keep2, powers, mode_rows, wide_rates, first_powers, partial,
    gates, rows_out, halo_rows, halo_out, halo_in, state_out, state_sent, state_in, incoming,
    gathered, total,
    load_sems, weight_sem, ready, halo_send, halo_recv, state_send, state_recv,
    sub_send, sub_recv, grp_send, grp_recv, fwd_send, fwd_recv,
):
    seq, grp, sub, reach_steps, pieces, groupings, trigger = sizes
    _, tokens, channels = x_ref.shape
    modes, groups = rates_ref.shape
    held = range(len(pieces) - 2, len(pieces))
    rows = channels // LANES
    pitch = gates.shape[0] // tokens
    group_size = channels // groups
    per_row = LANES // group_size
    steps = range(1, reach_steps + 1)
    z, g, s = lax.axis_index("seq"), lax.axis_index("grp"), lax.axis_index("sub")
    offset = z * tokens

    barrier = pltpu.get_barrier_semaphore()
    @pl.when(z > 0)
    def _():
        pl.semaphore_signal(barrier, inc=1, device_id={"seq": z - 1}, device_id_type=MESH)

    @pl.when(z < seq - 1)
    def _():
        pl.semaphore_signal(barrier, inc=1, device_id={"seq": z + 1}, device_id_type=MESH)

    for axis, me, count in (("grp", g, grp), ("sub", s, sub)):
        for step in range(1, count):
            pl.semaphore_signal(
                barrier, inc=1, device_id={axis: lax.rem(me + step, count)}, device_id_type=MESH
            )
    loads = [
        pltpu.make_async_copy(source, target, load_sems.at[i])
        for i, (source, target) in enumerate((
            (rates_hbm, rates_ref), (residues_hbm, residues_ref), (spans_hbm, spans_ref),
            (x_hbm.at[:, pl.ds(tokens - EDGE, EDGE), :], edge_ref), (taps_hbm, taps_ref),
            (x_hbm.at[pl.ds(1, 2)], x_ref.at[pl.ds(1, 2)]), (x_hbm.at[pl.ds(0, 1)], x_ref.at[pl.ds(0, 1)]),
        ))
    ]
    load_rates, load_residues, load_spans, load_edge, load_taps, load_kv, load_q = loads
    for load in loads:
        load.start()

    load_weight = pltpu.make_async_copy(weight_hbm, weight, weight_sem)
    load_weight.start()

    if pitch != rows:
        for buffer in (gates, mode_rows):
            buffer[...] = jnp.zeros_like(buffer)
    incoming[...] = jnp.zeros_like(incoming)
    for buffer in (wide_k, wide_v):
        buffer[:, pl.ds(0, HEAD), :] = jnp.zeros((rows, HEAD, LANES), F32)

    load_spans.wait()
    starts, start = [], jnp.int32(0)
    for i in range(spans_ref.shape[0]):
        starts.append(start)
        start = start + spans_ref[i]
    latest = jnp.int32(0)
    for first in starts:
        latest = jnp.where(first < offset + tokens, first, latest)
    position = offset - HEAD + lax.broadcasted_iota(jnp.int32, (tokens + HEAD, LANES), 0)
    here = position == starts[0]
    for first in starts[1:]:
        here = here | (position == first)
    keep1[...] = jnp.where(here, 0.0, 1.0)
    keep2[...] = keep1[pl.ds(HEAD, tokens), :] * keep1[pl.ds(HEAD - 1, tokens), :]

    load_rates.wait()
    load_residues.wait()
    rates = rates_ref[...]
    token = lax.broadcasted_iota(jnp.int32, (modes, tokens), 1)
    ahead = (token - (tokens - 1)).astype(F32)
    live = jnp.where((offset + token >= latest) & (token >= 2), 1.0, 0.0)
    for c in range(rows):
        for i in range(per_row):
            rate = jnp.broadcast_to(rates[:, c * per_row + i : c * per_row + i + 1], (modes, tokens))
            power = jnp.exp(rate * ahead) * live
            high = power.astype(BF16).astype(F32)
            wide_at = pl.ds(i * modes, modes)
            powers[c, wide_at, :] = high
            powers[c, pl.ds((per_row + i) * modes, modes), :] = power - high

    spread = (
        lax.broadcasted_iota(jnp.int32, (groups, channels), 1) // group_size
        == lax.broadcasted_iota(jnp.int32, (groups, channels), 0)
    ).astype(F32)
    drop = tanh(rates) * (1.0 + jnp.exp(-2.0 * rates))
    for first, values in ((0, rates), (modes, residues_ref[...] * jnp.sqrt(drop))):
        wide = jnp.dot(values, spread, precision=lax.Precision.HIGHEST, preferred_element_type=F32)
        if first == 0:
            wide_rates[...] = wide
            for t in range(2):
                first_live = jnp.where(offset + t >= latest, 1.0, 0.0)
                first_powers[t] = jnp.exp(wide * (-float(tokens - 1 - t))) * first_live
        for c in range(rows):
            mode_rows[pl.ds(first * pitch + c, modes, stride=pitch), :] = wide[
                :, c * LANES : (c + 1) * LANES
            ]

    load_edge.wait()
    for j in range(3):
        for c in range(rows):
            lanes = slice(c * LANES, (c + 1) * LANES)
            halo_rows[pl.ds(2 * j * pitch + c, 2, stride=pitch), :] = edge_ref[j, :, lanes].astype(F32)[EDGE - 2 :]
    halo_out[...] = halo_rows[...].astype(BF16)

    pl.semaphore_wait(barrier, jnp.minimum(seq - 1 - z, 1) + jnp.minimum(z, 1) + grp + sub - 2)

    send_halo = pltpu.make_async_remote_copy(
        src_ref=halo_out, dst_ref=halo_in, send_sem=halo_send, recv_sem=halo_recv,
        device_id={"seq": lax.rem(z + 1, seq)}, device_id_type=MESH,
    )

    @pl.when(z < seq - 1)
    def _():
        send_halo.start()

    def tell(step):
        @pl.when((z > 0) & (z + step - 1 < seq))
        def _():
            pl.semaphore_signal(
                ready.at[step - 1], inc=1, device_id={"seq": z - 1}, device_id_type=MESH
            )

    if reach_steps > 1:
        tell(2)

    load_taps.wait()

    def lanes_of(c):
        if isinstance(c, int):
            return slice(c * LANES, (c + 1) * LANES)
        return pl.ds(pl.multiple_of(c * LANES, LANES), LANES)

    def filtered(j, buffer, c, lower, count):
        tap = [taps_ref[k, pl.ds(j, 1), lanes_of(c)] for k in range(3)]
        now, last, older = (buffer[c, pl.ds(HEAD + lower - k, count), :] for k in range(3))
        m1, m2 = keep1[pl.ds(HEAD + lower, count), :], keep2[pl.ds(lower, count), :]
        return tap[0] * now + tap[1] * last * m1 + tap[2] * older * m2

    def gate(c, lower, count):
        value = (filtered(1, wide_k, c, lower, count) * filtered(2, wide_v, c, lower, count)).astype(BF16)
        gathered[0, pl.ds(lower, count), lanes_of(c)] = value
        gates[pl.ds(lower * pitch + c, count, stride=pitch), :] = value.astype(F32)

    load_kv.wait()
    block = 64

    def gate_rows(c, carry):
        for j, buffer in ((1, wide_k), (2, wide_v)):
            buffer[c, pl.ds(HEAD, tokens), :] = x_ref[j, :, lanes_of(c)].astype(F32)
        lower = 0
        while lower < tokens:
            count = min(block, tokens - lower)
            gate(c, lower, count)
            lower += count
        return carry

    lax.fori_loop(0, rows, gate_rows, 0)

    lane_group = lax.broadcasted_iota(jnp.int32, (modes, LANES), 1) // group_size
    for c in range(rows):
        lanes = slice(c * LANES, (c + 1) * LANES)
        sums = jnp.dot(powers[c].astype(BF16), gathered[0, :, lanes], preferred_element_type=F32)
        sums = sums[: per_row * modes] + sums[per_row * modes :]
        state = sums[:modes]
        for i in range(1, per_row):
            state = jnp.where(lane_group == i, sums[i * modes : (i + 1) * modes], state)
        partial[:, lanes] = state

    @pl.when(z == 0)
    def _():
        halo_in[...] = jnp.zeros_like(halo_in)

    @pl.when(z > 0)
    def _():
        send_halo.wait_recv()

    halo_rows[...] = halo_in[...].astype(F32)
    for j, buffer in enumerate((wide_q, wide_k, wide_v)):
        for c in range(rows):
            buffer[c, pl.ds(HEAD - 2, 2), :] = halo_rows[pl.ds(2 * j * pitch + c, 2, stride=pitch), :]
    for c in range(rows):
        lanes = slice(c * LANES, (c + 1) * LANES)
        value = filtered(1, wide_k, c, 0, HEAD) * filtered(2, wide_v, c, 0, HEAD)
        value = value.astype(BF16).astype(F32)
        gates[pl.ds(c, HEAD, stride=pitch), :] = value
        state = partial[:, lanes] + first_powers[0, :, lanes] * value[0:1] + first_powers[1, :, lanes] * value[1:2]
        half = c * 2 // rows
        state_out[pl.ds(half * modes, modes), slice((c - half * rows // 2) * LANES, (c - half * rows // 2 + 1) * LANES)] = state

    state_sent[...] = state_out[...].astype(BF16)
    state_copies = []
    for step in steps:
        copy = pltpu.make_async_remote_copy(
            src_ref=state_sent, dst_ref=state_in.at[step - 1],
            send_sem=state_send.at[step - 1], recv_sem=state_recv.at[step - 1],
            device_id={"seq": lax.rem(z + step, seq)}, device_id_type=MESH,
        )
        state_copies.append(copy)
    for step in steps:
        @pl.when(z + step < seq)
        def _():
            if step > 1:
                pl.semaphore_wait(ready.at[step - 1], 1)
            state_copies[step - 1].start()

        if 1 < step < reach_steps:
            tell(step + 1)

    def tile(ref, index):
        return ref[pl.ds(pl.multiple_of(index * pitch, pitch), pitch), :]

    decay = [jnp.exp(-tile(mode_rows, n)) for n in range(modes)]
    gain = [tile(mode_rows, modes + n) for n in range(modes)]
    load_q.wait()

    for step in steps:
        reach = (step - 1) * tokens
        open_ = jnp.float32(1.0)
        for first in starts:
            inside = (first >= offset - reach) & (first <= offset - 1)
            open_ = jnp.where(inside, 0.0, open_)

        @pl.when(z >= step)
        def _():
            state_copies[step - 1].wait_recv()
            came = state_in[step - 1].astype(F32)
            for c in range(rows):
                lanes = slice(c * LANES, (c + 1) * LANES)
                half = c * 2 // rows
                left = (c - half * rows // 2) * LANES
                part = came[half * modes : (half + 1) * modes, left : left + LANES] * open_
                if reach:
                    part = part * jnp.exp(wide_rates[:, lanes] * (-float(reach)))
                at = pl.ds(c, modes, stride=pitch)
                incoming[at, :] = incoming[at, :] + part

    own = g * sub + s
    carried = [tile(incoming, n) for n in range(modes)]
    unroll = 8

    def combine(parts):
        while len(parts) > 1:
            parts = [sum(parts[i + 1 : i + 2], parts[i]) for i in range(0, len(parts), 2)]
        return parts[0]

    def advance(block, state):
        for u in range(unroll):
            t = block * unroll + u
            gated, m1 = tile(gates, t), keep1[pl.ds(HEAD + t, 1), :]
            state = [decay[n] * (state[n] * m1) + gated for n in range(modes)]
            rows_out[pl.ds(pl.multiple_of(t * pitch, pitch), pitch), :] = combine(
                [gain[n] * state[n] for n in range(modes)]
            )
        return state

    def send(slot, c, axis, me, count, step, send_sem, recv_sem):
        lower, size, left, width = pieces[c]
        piece = gathered.at[1 + slot, pl.ds(lower, size), pl.ds(left, width)]
        return pltpu.make_async_remote_copy(
            src_ref=piece, dst_ref=piece, send_sem=send_sem, recv_sem=recv_sem,
            device_id={axis: lax.rem(me + step, count)}, device_id_type=MESH,
        )

    def over_sub(slot, c):
        return send(slot, c, "sub", s, sub, 1, sub_send.at[c], sub_recv.at[c])

    def over_grp(slot, c, step):
        return send(slot, c, "grp", g, grp, step, grp_send.at[step - 1, c], grp_recv.at[step - 1, c])

    def onward(slot, c, step):
        return send(slot, c, "sub", s, sub, 1, fwd_send.at[step - 1, c], fwd_recv.at[step - 1, c])

    for c, (lower, size, left, width) in enumerate(pieces):
        carried = carried if left else lax.fori_loop(lower // unroll, (lower + size) // unroll, advance, carried)

        def mix(r, carry):
            wide_q[r, pl.ds(HEAD + lower, size), :] = x_ref[0, pl.ds(lower, size), lanes_of(r)].astype(F32)
            long_out = rows_out[pl.ds(lower * pitch + r, size, stride=pitch), :]
            gathered[1 + own, pl.ds(lower, size), lanes_of(r)] = (
                filtered(0, wide_q, r, lower, size) * long_out
            ).astype(BF16)
            return carry

        if c == 0:
            for r in range(rows):
                mix(r, 0)
        else:
            lax.fori_loop(left // LANES, (left + width) // LANES, mix, 0)
        for step in range(1, grp):
            if c not in held:
                over_grp(own, c, step).start()
            else:
                pl.when(s == 0)(over_grp(own, c, step).start)
        over_sub(own, c).start()

    def product(slot, lower, count, left=0, width=channels):
        depth = pl.ds(pl.multiple_of(slot * channels + left, width), width)
        return jnp.dot(
            gathered[1 + slot, pl.ds(lower, count), pl.ds(left, width)], weight[depth, :],
            preferred_element_type=F32,
        )

    load_weight.wait()
    total[...] = product(own, 0, tokens)
    other = g * sub + 1 - s
    for c in range(len(pieces)):
        over_sub(other, c).wait_recv()
    total[...] += product(other, 0, tokens)

    def extent(members):
        return pieces[members[0]][0], sum(pieces[c][1] for c in members), *pieces[members[0]][2:]

    def direct(members):
        lower, count, left, width = extent(members)
        at = pl.ds(lower, count)
        for step in range(1, grp):
            slot = lax.rem(g + grp - step, grp) * sub + s
            for c in members:
                over_grp(slot, c, step).wait_recv()
                onward(slot, c, step).start()
            total[at, :] += product(slot, lower, count, left, width)

    def forwarded(members):
        lower, count, left, width = extent(members)
        at = pl.ds(lower, count)
        for step in range(1, grp):
            slot = lax.rem(g + grp - step, grp) * sub + 1 - s
            for c in members:
                onward(slot, c, step).wait_recv()
                if step == 1 and c == trigger:
                    @pl.when(s == 1)
                    def _():
                        for late in held:
                            for way in range(1, grp):
                                over_grp(own, late, way).start()
            value = total[at, :] + product(slot, lower, count, left, width)
            if step < grp - 1 or left + width < channels:
                total[at, :] = value
            else:
                out_ref[at, :] = value.astype(out_ref.dtype)

    for members in groupings[:-2]:
        direct(members)
        forwarded(members)
    for members in groupings[-2:]:
        direct(members)
    for members in groupings[-2:]:
        forwarded(members)

    for step in range(1, grp):
        for c in range(len(pieces)):
            over_grp(own, c, step).wait_send()
            onward(own, c, step).wait_send()
    for c in range(len(pieces)):
        over_sub(own, c).wait_send()
    pl.when(z < seq - 1)(send_halo.wait_send)
    for step in steps:
        pl.when(z + step < seq)(state_copies[step - 1].wait_send)


def shards(sizes, projected, short_filter, span_lengths, mode_rates, mode_residues, out_weight):
    seq, grp, sub = sizes
    tokens, _, channels = projected.shape
    modes, groups = mode_rates.shape
    rows = channels // LANES
    pitch = -(-rows // 8) * 8
    reach_steps = min(seq - 1, (seq * tokens // 2 - 1 + tokens - 1) // tokens)
    sizes_of = (16, 48, 32, 32, 64, 64)
    pieces = [(sum(sizes_of[:i]), size, 0, channels) for i, size in enumerate(sizes_of)]
    lower, size, left, width = pieces.pop()
    half = width // 2
    pieces = (*pieces, (lower, size, 0, half), (lower, size, half, half))
    count = len(pieces)
    groupings, trigger = ((0, 1, 2, 3), (4,), (5,), (6,)), 3
    per_row = LANES * groups // channels
    streams = projected.transpose(1, 0, 2)
    vmem = pl.BlockSpec(memory_space=pltpu.VMEM)
    hbm = pl.BlockSpec(memory_space=pl.ANY)
    dma = pltpu.SemaphoreType.DMA
    row_tile = pltpu.VMEM((tokens * pitch, LANES), F32)
    stream = pltpu.VMEM((rows, tokens + HEAD, LANES), F32)
    state, packed = (modes, channels), (2 * modes, channels // 2)
    return pl.pallas_call(
        functools.partial(kernel, (seq, grp, sub, reach_steps, pieces, groupings, trigger)),
        out_shape=pltpu.VMEM((tokens, out_weight.shape[1]), BF16),
        in_specs=[hbm] * 6,
        out_specs=vmem,
        scratch_shapes=[
            pltpu.SMEM(span_lengths.shape, jnp.int32),
            pltpu.VMEM(streams.shape, BF16),
            pltpu.VMEM((3, EDGE, channels), BF16),
            pltpu.VMEM(short_filter.shape, F32),
            pltpu.VMEM(mode_rates.shape, F32),
            pltpu.VMEM(mode_residues.shape, F32),
            pltpu.VMEM(out_weight.shape, BF16),
            stream, stream, stream,
            pltpu.VMEM((tokens + HEAD, LANES), F32),
            pltpu.VMEM((tokens, LANES), F32),
            pltpu.VMEM((rows, 2 * per_row * modes, tokens), F32),
            pltpu.VMEM((2 * modes * pitch, LANES), F32),
            pltpu.VMEM(state, F32),
            pltpu.VMEM((2,) + state, F32),
            pltpu.VMEM(state, F32),
            row_tile, row_tile,
            pltpu.VMEM((6 * pitch, LANES), F32),
            pltpu.VMEM((6 * pitch, LANES), BF16),
            pltpu.VMEM((6 * pitch, LANES), BF16),
            pltpu.VMEM(packed, F32),
            pltpu.VMEM(packed, BF16),
            pltpu.VMEM((reach_steps,) + packed, BF16),
            pltpu.VMEM((modes * pitch, LANES), F32),
            pltpu.VMEM((1 + grp * sub, tokens, channels), BF16),
            pltpu.VMEM((tokens, out_weight.shape[1]), F32),
            dma((7,)), dma, pltpu.SemaphoreType.REGULAR((reach_steps,)), dma, dma,
            dma((reach_steps,)), dma((reach_steps,)),
            dma((count,)), dma((count,)),
            dma((grp - 1, count)), dma((grp - 1, count)),
            dma((grp - 1, count)), dma((grp - 1, count)),
        ],
        compiler_params=pltpu.CompilerParams(collective_id=0, has_side_effects=True),
    )(span_lengths, streams, short_filter, mode_rates, mode_residues, out_weight)


def solution(mesh):
    sizes = (mesh.shape["seq"], mesh.shape["grp"], mesh.shape["sub"])
    return jax.shard_map(
        functools.partial(shards, sizes),
        mesh=mesh,
        in_specs=(
            P(("parts", "seq"), None, ("grp", "sub")),
            P(None, None, ("grp", "sub")),
            P("parts"),
            P(None, ("grp", "sub")),
            P(None, ("grp", "sub")),
            P(None, ("grp", "sub")),
        ),
        out_specs=P(("parts", "seq"), ("grp", "sub")),
        check_vma=False,
    )
```

```python
import functools

import jax
import jax.numpy as jnp
from jax import lax
from jax.experimental import pallas as pl
from jax.experimental.pallas import tpu as pltpu
from jax.sharding import PartitionSpec as P

MESH = pl.DeviceIdType.MESH
LANES = 128
HEAD = 8
EDGE = 16
F32, BF16 = jnp.float32, jnp.bfloat16


def tanh(x):
    x = jnp.clip(x, -7.90531110763549805, 7.90531110763549805)
    square = x * x
    top = jnp.full_like(x, -2.76076847742355e-16)
    for c in (
        2.00018790482477e-13, -8.60467152213735e-11, 5.12229709037114e-08,
        1.48572235717979e-05, 6.37261928875436e-04, 4.89352455891786e-03,
    ):
        top = top * square + c
    bottom = jnp.full_like(x, 1.19825839466702e-06)
    for c in (1.18534705686654e-04, 2.26843463243900e-03, 4.89352518554385e-03):
        bottom = bottom * square + c
    return jnp.where(jnp.abs(x) < 0.0004, x, x * top / bottom)


def kernel(
    sizes, spans_hbm, x_hbm, taps_hbm, rates_hbm, residues_hbm, weight_hbm, out_ref,
    spans_ref, x_ref, edge_ref, taps_ref, rates_ref, residues_ref, weight,
    wide_q, wide_k, wide_v, keep1, keep2, powers, mode_rows, wide_rates, first_powers, partial,
    gates, rows_out, halo_rows, halo_out, halo_in, state_out, state_sent, state_in, incoming,
    gathered, total,
    load_sems, weight_sem, ready, halo_send, halo_recv, state_send, state_recv,
    sub_send, sub_recv, grp_send, grp_recv, fwd_send, fwd_recv,
):
    seq, grp, sub, reach_steps, pieces, groupings, trigger = sizes
    _, tokens, channels = x_ref.shape
    modes, groups = rates_ref.shape
    held = range(len(pieces) - 2, len(pieces))
    rows = channels // LANES
    pitch = gates.shape[0] // tokens
    group_size = channels // groups
    per_row = LANES // group_size
    steps = range(1, reach_steps + 1)
    z, g, s = lax.axis_index("seq"), lax.axis_index("grp"), lax.axis_index("sub")
    offset = z * tokens

    barrier = pltpu.get_barrier_semaphore()
    @pl.when(z > 0)
    def _():
        pl.semaphore_signal(barrier, inc=1, device_id={"seq": z - 1}, device_id_type=MESH)

    @pl.when(z < seq - 1)
    def _():
        pl.semaphore_signal(barrier, inc=1, device_id={"seq": z + 1}, device_id_type=MESH)

    for axis, me, count in (("grp", g, grp), ("sub", s, sub)):
        for step in range(1, count):
            pl.semaphore_signal(
                barrier, inc=1, device_id={axis: lax.rem(me + step, count)}, device_id_type=MESH
            )
    loads = [
        pltpu.make_async_copy(source, target, load_sems.at[i])
        for i, (source, target) in enumerate((
            (rates_hbm, rates_ref), (residues_hbm, residues_ref), (spans_hbm, spans_ref),
            (x_hbm.at[:, pl.ds(tokens - EDGE, EDGE), :], edge_ref), (taps_hbm, taps_ref),
            (x_hbm.at[pl.ds(1, 2)], x_ref.at[pl.ds(1, 2)]), (x_hbm.at[pl.ds(0, 1)], x_ref.at[pl.ds(0, 1)]),
        ))
    ]
    load_rates, load_residues, load_spans, load_edge, load_taps, load_kv, load_q = loads
    for load in loads:
        load.start()

    load_weight = pltpu.make_async_copy(weight_hbm, weight, weight_sem)
    load_weight.start()

    if pitch != rows:
        for buffer in (gates, mode_rows):
            buffer[...] = jnp.zeros_like(buffer)
    incoming[...] = jnp.zeros_like(incoming)
    for buffer in (wide_k, wide_v):
        buffer[:, pl.ds(0, HEAD), :] = jnp.zeros((rows, HEAD, LANES), F32)

    load_spans.wait()
    starts, start = [], jnp.int32(0)
    for i in range(spans_ref.shape[0]):
        starts.append(start)
        start = start + spans_ref[i]
    latest = jnp.int32(0)
    for first in starts:
        latest = jnp.where(first < offset + tokens, first, latest)
    position = offset - HEAD + lax.broadcasted_iota(jnp.int32, (tokens + HEAD, LANES), 0)
    here = position == starts[0]
    for first in starts[1:]:
        here = here | (position == first)
    keep1[...] = jnp.where(here, 0.0, 1.0)
    keep2[...] = keep1[pl.ds(HEAD, tokens), :] * keep1[pl.ds(HEAD - 1, tokens), :]

    load_rates.wait()
    load_residues.wait()
    rates = rates_ref[...]
    token = lax.broadcasted_iota(jnp.int32, (modes, tokens), 1)
    ahead = (token - (tokens - 1)).astype(F32)
    live = jnp.where((offset + token >= latest) & (token >= 2), 1.0, 0.0)
    for c in range(rows):
        for i in range(per_row):
            rate = jnp.broadcast_to(rates[:, c * per_row + i : c * per_row + i + 1], (modes, tokens))
            power = jnp.exp(rate * ahead) * live
            high = power.astype(BF16).astype(F32)
            wide_at = pl.ds(i * modes, modes)
            powers[c, wide_at, :] = high
            powers[c, pl.ds((per_row + i) * modes, modes), :] = power - high

    spread = (
        lax.broadcasted_iota(jnp.int32, (groups, channels), 1) // group_size
        == lax.broadcasted_iota(jnp.int32, (groups, channels), 0)
    ).astype(F32)
    drop = tanh(rates) * (1.0 + jnp.exp(-2.0 * rates))
    for first, values in ((0, rates), (modes, residues_ref[...] * jnp.sqrt(drop))):
        wide = jnp.dot(values, spread, precision=lax.Precision.HIGHEST, preferred_element_type=F32)
        if first == 0:
            wide_rates[...] = wide
            for t in range(2):
                first_live = jnp.where(offset + t >= latest, 1.0, 0.0)
                first_powers[t] = jnp.exp(wide * (-float(tokens - 1 - t))) * first_live
        for c in range(rows):
            mode_rows[pl.ds(first * pitch + c, modes, stride=pitch), :] = wide[
                :, c * LANES : (c + 1) * LANES
            ]

    load_edge.wait()
    for j in range(3):
        for c in range(rows):
            lanes = slice(c * LANES, (c + 1) * LANES)
            halo_rows[pl.ds(2 * j * pitch + c, 2, stride=pitch), :] = edge_ref[j, :, lanes].astype(F32)[EDGE - 2 :]
    halo_out[...] = halo_rows[...].astype(BF16)

    pl.semaphore_wait(barrier, jnp.minimum(seq - 1 - z, 1) + jnp.minimum(z, 1) + grp + sub - 2)

    send_halo = pltpu.make_async_remote_copy(
        src_ref=halo_out, dst_ref=halo_in, send_sem=halo_send, recv_sem=halo_recv,
        device_id={"seq": lax.rem(z + 1, seq)}, device_id_type=MESH,
    )

    @pl.when(z < seq - 1)
    def _():
        send_halo.start()

    def tell(step):
        @pl.when((z > 0) & (z + step - 1 < seq))
        def _():
            pl.semaphore_signal(
                ready.at[step - 1], inc=1, device_id={"seq": z - 1}, device_id_type=MESH
            )

    if reach_steps > 1:
        tell(2)

    load_taps.wait()

    def lanes_of(c):
        if isinstance(c, int):
            return slice(c * LANES, (c + 1) * LANES)
        return pl.ds(pl.multiple_of(c * LANES, LANES), LANES)

    def filtered(j, buffer, c, lower, count):
        tap = [taps_ref[k, pl.ds(j, 1), lanes_of(c)] for k in range(3)]
        now, last, older = (buffer[c, pl.ds(HEAD + lower - k, count), :] for k in range(3))
        m1, m2 = keep1[pl.ds(HEAD + lower, count), :], keep2[pl.ds(lower, count), :]
        return tap[0] * now + tap[1] * last * m1 + tap[2] * older * m2

    def gate(c, lower, count):
        value = (filtered(1, wide_k, c, lower, count) * filtered(2, wide_v, c, lower, count)).astype(BF16)
        gathered[0, pl.ds(lower, count), lanes_of(c)] = value
        gates[pl.ds(lower * pitch + c, count, stride=pitch), :] = value.astype(F32)

    load_kv.wait()
    block = 64

    def gate_rows(c, carry):
        for j, buffer in ((1, wide_k), (2, wide_v)):
            buffer[c, pl.ds(HEAD, tokens), :] = x_ref[j, :, lanes_of(c)].astype(F32)
        lower = 0
        while lower < tokens:
            count = min(block, tokens - lower)
            gate(c, lower, count)
            lower += count
        return carry

    lax.fori_loop(0, rows, gate_rows, 0)

    lane_group = lax.broadcasted_iota(jnp.int32, (modes, LANES), 1) // group_size
    for c in range(rows):
        lanes = slice(c * LANES, (c + 1) * LANES)
        sums = jnp.dot(powers[c].astype(BF16), gathered[0, :, lanes], preferred_element_type=F32)
        sums = sums[: per_row * modes] + sums[per_row * modes :]
        state = sums[:modes]
        for i in range(1, per_row):
            state = jnp.where(lane_group == i, sums[i * modes : (i + 1) * modes], state)
        partial[:, lanes] = state

    @pl.when(z == 0)
    def _():
        halo_in[...] = jnp.zeros_like(halo_in)

    @pl.when(z > 0)
    def _():
        send_halo.wait_recv()

    halo_rows[...] = halo_in[...].astype(F32)
    for j, buffer in enumerate((wide_q, wide_k, wide_v)):
        for c in range(rows):
            buffer[c, pl.ds(HEAD - 2, 2), :] = halo_rows[pl.ds(2 * j * pitch + c, 2, stride=pitch), :]
    for c in range(rows):
        lanes = slice(c * LANES, (c + 1) * LANES)
        value = filtered(1, wide_k, c, 0, HEAD) * filtered(2, wide_v, c, 0, HEAD)
        value = value.astype(BF16).astype(F32)
        gates[pl.ds(c, HEAD, stride=pitch), :] = value
        state = partial[:, lanes] + first_powers[0, :, lanes] * value[0:1] + first_powers[1, :, lanes] * value[1:2]
        half = c * 2 // rows
        state_out[pl.ds(half * modes, modes), slice((c - half * rows // 2) * LANES, (c - half * rows // 2 + 1) * LANES)] = state

    state_sent[...] = state_out[...].astype(BF16)
    state_copies = []
    for step in steps:
        copy = pltpu.make_async_remote_copy(
            src_ref=state_sent, dst_ref=state_in.at[step - 1],
            send_sem=state_send.at[step - 1], recv_sem=state_recv.at[step - 1],
            device_id={"seq": lax.rem(z + step, seq)}, device_id_type=MESH,
        )
        state_copies.append(copy)
    for step in steps:
        @pl.when(z + step < seq)
        def _():
            if step > 1:
                pl.semaphore_wait(ready.at[step - 1], 1)
            state_copies[step - 1].start()

        if 1 < step < reach_steps:
            tell(step + 1)

    def tile(ref, index):
        return ref[pl.ds(pl.multiple_of(index * pitch, pitch), pitch), :]

    decay = [jnp.exp(-tile(mode_rows, n)) for n in range(modes)]
    gain = [tile(mode_rows, modes + n) for n in range(modes)]
    load_q.wait()

    for step in steps:
        reach = (step - 1) * tokens
        open_ = jnp.float32(1.0)
        for first in starts:
            inside = (first >= offset - reach) & (first <= offset - 1)
            open_ = jnp.where(inside, 0.0, open_)

        @pl.when(z >= step)
        def _():
            state_copies[step - 1].wait_recv()
            came = state_in[step - 1].astype(F32)
            for c in range(rows):
                lanes = slice(c * LANES, (c + 1) * LANES)
                half = c * 2 // rows
                left = (c - half * rows // 2) * LANES
                part = came[half * modes : (half + 1) * modes, left : left + LANES] * open_
                if reach:
                    part = part * jnp.exp(wide_rates[:, lanes] * (-float(reach)))
                at = pl.ds(c, modes, stride=pitch)
                incoming[at, :] = incoming[at, :] + part

    own = g * sub + s
    carried = [tile(incoming, n) for n in range(modes)]
    unroll = 8

    def combine(parts):
        while len(parts) > 1:
            parts = [sum(parts[i + 1 : i + 2], parts[i]) for i in range(0, len(parts), 2)]
        return parts[0]

    def advance(block, state):
        for u in range(unroll):
            t = block * unroll + u
            gated, m1 = tile(gates, t), keep1[pl.ds(HEAD + t, 1), :]
            state = [decay[n] * (state[n] * m1) + gated for n in range(modes)]
            rows_out[pl.ds(pl.multiple_of(t * pitch, pitch), pitch), :] = combine(
                [gain[n] * state[n] for n in range(modes)]
            )
        return state

    def send(slot, c, axis, me, count, step, send_sem, recv_sem):
        lower, size, left, width = pieces[c]
        piece = gathered.at[1 + slot, pl.ds(lower, size), pl.ds(left, width)]
        return pltpu.make_async_remote_copy(
            src_ref=piece, dst_ref=piece, send_sem=send_sem, recv_sem=recv_sem,
            device_id={axis: lax.rem(me + step, count)}, device_id_type=MESH,
        )

    def over_sub(slot, c):
        return send(slot, c, "sub", s, sub, 1, sub_send.at[c], sub_recv.at[c])

    def over_grp(slot, c, step):
        return send(slot, c, "grp", g, grp, step, grp_send.at[step - 1, c], grp_recv.at[step - 1, c])

    def onward(slot, c, step):
        return send(slot, c, "sub", s, sub, 1, fwd_send.at[step - 1, c], fwd_recv.at[step - 1, c])

    for c, (lower, size, left, width) in enumerate(pieces):
        carried = carried if left else lax.fori_loop(lower // unroll, (lower + size) // unroll, advance, carried)

        def mix(r, carry):
            wide_q[r, pl.ds(HEAD + lower, size), :] = x_ref[0, pl.ds(lower, size), lanes_of(r)].astype(F32)
            long_out = rows_out[pl.ds(lower * pitch + r, size, stride=pitch), :]
            gathered[1 + own, pl.ds(lower, size), lanes_of(r)] = (
                filtered(0, wide_q, r, lower, size) * long_out
            ).astype(BF16)
            return carry

        if c == 0:
            for r in range(rows):
                mix(r, 0)
        else:
            lax.fori_loop(left // LANES, (left + width) // LANES, mix, 0)
        for step in range(1, grp):
            if c not in held:
                over_grp(own, c, step).start()
            else:
                pl.when(s == 0)(over_grp(own, c, step).start)
        over_sub(own, c).start()

    def product(slot, lower, count, left=0, width=channels):
        depth = pl.ds(pl.multiple_of(slot * channels + left, width), width)
        return jnp.dot(
            gathered[1 + slot, pl.ds(lower, count), pl.ds(left, width)], weight[depth, :],
            preferred_element_type=F32,
        )

    load_weight.wait()
    total[...] = product(own, 0, tokens)
    other = g * sub + 1 - s
    for c in range(len(pieces)):
        over_sub(other, c).wait_recv()
    total[...] += product(other, 0, tokens)

    def extent(members):
        return pieces[members[0]][0], sum(pieces[c][1] for c in members), *pieces[members[0]][2:]

    def direct(members):
        lower, count, left, width = extent(members)
        at = pl.ds(lower, count)
        for step in range(1, grp):
            slot = lax.rem(g + grp - step, grp) * sub + s
            for c in members:
                over_grp(slot, c, step).wait_recv()
                onward(slot, c, step).start()
            total[at, :] += product(slot, lower, count, left, width)

    def forwarded(members):
        lower, count, left, width = extent(members)
        at = pl.ds(lower, count)
        for step in range(1, grp):
            slot = lax.rem(g + grp - step, grp) * sub + 1 - s
            for c in members:
                onward(slot, c, step).wait_recv()
                if step == 1 and c == trigger:
                    @pl.when(s == 1)
                    def _():
                        for late in held:
                            for way in range(1, grp):
                                over_grp(own, late, way).start()
            value = total[at, :] + product(slot, lower, count, left, width)
            if step < grp - 1 or left + width < channels:
                total[at, :] = value
            else:
                out_ref[at, :] = value.astype(out_ref.dtype)

    for members in groupings[:-2]:
        direct(members)
        forwarded(members)
    for members in groupings[-2:]:
        direct(members)
    for members in groupings[-2:]:
        forwarded(members)

    for step in range(1, grp):
        for c in range(len(pieces)):
            over_grp(own, c, step).wait_send()
            onward(own, c, step).wait_send()
    for c in range(len(pieces)):
        over_sub(own, c).wait_send()
    pl.when(z < seq - 1)(send_halo.wait_send)
    for step in steps:
        pl.when(z + step < seq)(state_copies[step - 1].wait_send)


def shards(sizes, projected, short_filter, span_lengths, mode_rates, mode_residues, out_weight):
    seq, grp, sub = sizes
    tokens, _, channels = projected.shape
    modes, groups = mode_rates.shape
    rows = channels // LANES
    pitch = -(-rows // 8) * 8
    reach_steps = min(seq - 1, (seq * tokens // 2 - 1 + tokens - 1) // tokens)
    sizes_of = (16, 16, 32, 64, 64, 64)
    pieces = [(sum(sizes_of[:i]), size, 0, channels) for i, size in enumerate(sizes_of)]
    lower, size, left, width = pieces.pop()
    half = width // 2
    pieces = (*pieces, (lower, size, 0, half), (lower, size, half, half))
    count = len(pieces)
    groupings, trigger = ((0, 1, 2, 3), (4,), (5,), (6,)), 3
    per_row = LANES * groups // channels
    streams = projected.transpose(1, 0, 2)
    vmem = pl.BlockSpec(memory_space=pltpu.VMEM)
    hbm = pl.BlockSpec(memory_space=pl.ANY)
    dma = pltpu.SemaphoreType.DMA
    row_tile = pltpu.VMEM((tokens * pitch, LANES), F32)
    stream = pltpu.VMEM((rows, tokens + HEAD, LANES), F32)
    state, packed = (modes, channels), (2 * modes, channels // 2)
    return pl.pallas_call(
        functools.partial(kernel, (seq, grp, sub, reach_steps, pieces, groupings, trigger)),
        out_shape=pltpu.VMEM((tokens, out_weight.shape[1]), BF16),
        in_specs=[hbm] * 6,
        out_specs=vmem,
        scratch_shapes=[
            pltpu.SMEM(span_lengths.shape, jnp.int32),
            pltpu.VMEM(streams.shape, BF16),
            pltpu.VMEM((3, EDGE, channels), BF16),
            pltpu.VMEM(short_filter.shape, F32),
            pltpu.VMEM(mode_rates.shape, F32),
            pltpu.VMEM(mode_residues.shape, F32),
            pltpu.VMEM(out_weight.shape, BF16),
            stream, stream, stream,
            pltpu.VMEM((tokens + HEAD, LANES), F32),
            pltpu.VMEM((tokens, LANES), F32),
            pltpu.VMEM((rows, 2 * per_row * modes, tokens), F32),
            pltpu.VMEM((2 * modes * pitch, LANES), F32),
            pltpu.VMEM(state, F32),
            pltpu.VMEM((2,) + state, F32),
            pltpu.VMEM(state, F32),
            row_tile, row_tile,
            pltpu.VMEM((6 * pitch, LANES), F32),
            pltpu.VMEM((6 * pitch, LANES), BF16),
            pltpu.VMEM((6 * pitch, LANES), BF16),
            pltpu.VMEM(packed, F32),
            pltpu.VMEM(packed, BF16),
            pltpu.VMEM((reach_steps,) + packed, BF16),
            pltpu.VMEM((modes * pitch, LANES), F32),
            pltpu.VMEM((1 + grp * sub, tokens, channels), BF16),
            pltpu.VMEM((tokens, out_weight.shape[1]), F32),
            dma((7,)), dma, pltpu.SemaphoreType.REGULAR((reach_steps,)), dma, dma,
            dma((reach_steps,)), dma((reach_steps,)),
            dma((count,)), dma((count,)),
            dma((grp - 1, count)), dma((grp - 1, count)),
            dma((grp - 1, count)), dma((grp - 1, count)),
        ],
        compiler_params=pltpu.CompilerParams(collective_id=0, has_side_effects=True),
    )(span_lengths, streams, short_filter, mode_rates, mode_residues, out_weight)


def solution(mesh):
    sizes = (mesh.shape["seq"], mesh.shape["grp"], mesh.shape["sub"])
    return jax.shard_map(
        functools.partial(shards, sizes),
        mesh=mesh,
        in_specs=(
            P(("parts", "seq"), None, ("grp", "sub")),
            P(None, None, ("grp", "sub")),
            P("parts"),
            P(None, ("grp", "sub")),
            P(None, ("grp", "sub")),
            P(None, ("grp", "sub")),
        ),
        out_specs=P(("parts", "seq"), ("grp", "sub")),
        check_vma=False,
    )
```

```python
import functools

import jax
import jax.numpy as jnp
from jax import lax
from jax.experimental import pallas as pl
from jax.experimental.pallas import tpu as pltpu
from jax.sharding import PartitionSpec as P

MESH = pl.DeviceIdType.MESH
LANES = 128
HEAD = 8
EDGE = 16
F32, BF16 = jnp.float32, jnp.bfloat16


def tanh(x):
    x = jnp.clip(x, -7.90531110763549805, 7.90531110763549805)
    square = x * x
    top = jnp.full_like(x, -2.76076847742355e-16)
    for c in (
        2.00018790482477e-13, -8.60467152213735e-11, 5.12229709037114e-08,
        1.48572235717979e-05, 6.37261928875436e-04, 4.89352455891786e-03,
    ):
        top = top * square + c
    bottom = jnp.full_like(x, 1.19825839466702e-06)
    for c in (1.18534705686654e-04, 2.26843463243900e-03, 4.89352518554385e-03):
        bottom = bottom * square + c
    return jnp.where(jnp.abs(x) < 0.0004, x, x * top / bottom)


def kernel(
    sizes, spans_hbm, x_hbm, taps_hbm, rates_hbm, residues_hbm, weight_hbm, out_ref,
    spans_ref, x_ref, edge_ref, taps_ref, rates_ref, residues_ref, weight,
    wide_q, wide_k, wide_v, keep1, keep2, powers, mode_rows, wide_rates, first_powers, partial,
    gates, rows_out, halo_rows, halo_out, halo_in, state_out, state_sent, state_in, incoming,
    gathered, total,
    load_sems, weight_sem, ready, halo_send, halo_recv, state_send, state_recv,
    sub_send, sub_recv, grp_send, grp_recv, fwd_send, fwd_recv,
):
    seq, grp, sub, reach_steps, pieces, groupings, trigger = sizes
    _, tokens, channels = x_ref.shape
    modes, groups = rates_ref.shape
    held = range(len(pieces) - 2, len(pieces))
    rows = channels // LANES
    pitch = gates.shape[0] // tokens
    group_size = channels // groups
    per_row = LANES // group_size
    steps = range(1, reach_steps + 1)
    z, g, s = lax.axis_index("seq"), lax.axis_index("grp"), lax.axis_index("sub")
    offset = z * tokens

    barrier = pltpu.get_barrier_semaphore()
    @pl.when(z > 0)
    def _():
        pl.semaphore_signal(barrier, inc=1, device_id={"seq": z - 1}, device_id_type=MESH)

    @pl.when(z < seq - 1)
    def _():
        pl.semaphore_signal(barrier, inc=1, device_id={"seq": z + 1}, device_id_type=MESH)

    for axis, me, count in (("grp", g, grp), ("sub", s, sub)):
        for step in range(1, count):
            pl.semaphore_signal(
                barrier, inc=1, device_id={axis: lax.rem(me + step, count)}, device_id_type=MESH
            )
    loads = [
        pltpu.make_async_copy(source, target, load_sems.at[i])
        for i, (source, target) in enumerate((
            (rates_hbm, rates_ref), (residues_hbm, residues_ref), (spans_hbm, spans_ref),
            (x_hbm.at[:, pl.ds(tokens - EDGE, EDGE), :], edge_ref), (taps_hbm, taps_ref),
            (x_hbm.at[pl.ds(1, 2)], x_ref.at[pl.ds(1, 2)]), (x_hbm.at[pl.ds(0, 1)], x_ref.at[pl.ds(0, 1)]),
        ))
    ]
    load_rates, load_residues, load_spans, load_edge, load_taps, load_kv, load_q = loads
    for load in loads:
        load.start()

    load_weight = pltpu.make_async_copy(weight_hbm, weight, weight_sem)
    load_weight.start()

    if pitch != rows:
        for buffer in (gates, mode_rows):
            buffer[...] = jnp.zeros_like(buffer)
    incoming[...] = jnp.zeros_like(incoming)
    for buffer in (wide_k, wide_v):
        buffer[:, pl.ds(0, HEAD), :] = jnp.zeros((rows, HEAD, LANES), F32)

    load_spans.wait()
    starts, start = [], jnp.int32(0)
    for i in range(spans_ref.shape[0]):
        starts.append(start)
        start = start + spans_ref[i]
    latest = jnp.int32(0)
    for first in starts:
        latest = jnp.where(first < offset + tokens, first, latest)
    position = offset - HEAD + lax.broadcasted_iota(jnp.int32, (tokens + HEAD, LANES), 0)
    here = position == starts[0]
    for first in starts[1:]:
        here = here | (position == first)
    keep1[...] = jnp.where(here, 0.0, 1.0)
    keep2[...] = keep1[pl.ds(HEAD, tokens), :] * keep1[pl.ds(HEAD - 1, tokens), :]

    load_rates.wait()
    load_residues.wait()
    rates = rates_ref[...]
    token = lax.broadcasted_iota(jnp.int32, (modes, tokens), 1)
    ahead = (token - (tokens - 1)).astype(F32)
    live = jnp.where((offset + token >= latest) & (token >= 2), 1.0, 0.0)
    for c in range(rows):
        for i in range(per_row):
            rate = jnp.broadcast_to(rates[:, c * per_row + i : c * per_row + i + 1], (modes, tokens))
            power = jnp.exp(rate * ahead) * live
            high = power.astype(BF16).astype(F32)
            wide_at = pl.ds(i * modes, modes)
            powers[c, wide_at, :] = high
            powers[c, pl.ds((per_row + i) * modes, modes), :] = power - high

    spread = (
        lax.broadcasted_iota(jnp.int32, (groups, channels), 1) // group_size
        == lax.broadcasted_iota(jnp.int32, (groups, channels), 0)
    ).astype(F32)
    drop = tanh(rates) * (1.0 + jnp.exp(-2.0 * rates))
    for first, values in ((0, rates), (modes, residues_ref[...] * jnp.sqrt(drop))):
        wide = jnp.dot(values, spread, precision=lax.Precision.HIGHEST, preferred_element_type=F32)
        if first == 0:
            wide_rates[...] = wide
            for t in range(2):
                first_live = jnp.where(offset + t >= latest, 1.0, 0.0)
                first_powers[t] = jnp.exp(wide * (-float(tokens - 1 - t))) * first_live
        for c in range(rows):
            mode_rows[pl.ds(first * pitch + c, modes, stride=pitch), :] = wide[
                :, c * LANES : (c + 1) * LANES
            ]

    load_edge.wait()
    for j in range(3):
        for c in range(rows):
            lanes = slice(c * LANES, (c + 1) * LANES)
            halo_rows[pl.ds(2 * j * pitch + c, 2, stride=pitch), :] = edge_ref[j, :, lanes].astype(F32)[EDGE - 2 :]
    halo_out[...] = halo_rows[...].astype(BF16)

    pl.semaphore_wait(barrier, jnp.minimum(seq - 1 - z, 1) + jnp.minimum(z, 1) + grp + sub - 2)

    send_halo = pltpu.make_async_remote_copy(
        src_ref=halo_out, dst_ref=halo_in, send_sem=halo_send, recv_sem=halo_recv,
        device_id={"seq": lax.rem(z + 1, seq)}, device_id_type=MESH,
    )

    @pl.when(z < seq - 1)
    def _():
        send_halo.start()

    def tell(step):
        @pl.when((z > 0) & (z + step - 1 < seq))
        def _():
            pl.semaphore_signal(
                ready.at[step - 1], inc=1, device_id={"seq": z - 1}, device_id_type=MESH
            )

    if reach_steps > 1:
        tell(2)

    load_taps.wait()

    def lanes_of(c):
        if isinstance(c, int):
            return slice(c * LANES, (c + 1) * LANES)
        return pl.ds(pl.multiple_of(c * LANES, LANES), LANES)

    def filtered(j, buffer, c, lower, count):
        tap = [taps_ref[k, pl.ds(j, 1), lanes_of(c)] for k in range(3)]
        now, last, older = (buffer[c, pl.ds(HEAD + lower - k, count), :] for k in range(3))
        m1, m2 = keep1[pl.ds(HEAD + lower, count), :], keep2[pl.ds(lower, count), :]
        return tap[0] * now + tap[1] * last * m1 + tap[2] * older * m2

    def gate(c, lower, count):
        value = (filtered(1, wide_k, c, lower, count) * filtered(2, wide_v, c, lower, count)).astype(BF16)
        gathered[0, pl.ds(lower, count), lanes_of(c)] = value
        gates[pl.ds(lower * pitch + c, count, stride=pitch), :] = value.astype(F32)

    load_kv.wait()
    block = 64

    def gate_rows(c, carry):
        for j, buffer in ((1, wide_k), (2, wide_v)):
            buffer[c, pl.ds(HEAD, tokens), :] = x_ref[j, :, lanes_of(c)].astype(F32)
        lower = 0
        while lower < tokens:
            count = min(block, tokens - lower)
            gate(c, lower, count)
            lower += count
        return carry

    lax.fori_loop(0, rows, gate_rows, 0)

    lane_group = lax.broadcasted_iota(jnp.int32, (modes, LANES), 1) // group_size
    for c in range(rows):
        lanes = slice(c * LANES, (c + 1) * LANES)
        sums = jnp.dot(powers[c].astype(BF16), gathered[0, :, lanes], preferred_element_type=F32)
        sums = sums[: per_row * modes] + sums[per_row * modes :]
        state = sums[:modes]
        for i in range(1, per_row):
            state = jnp.where(lane_group == i, sums[i * modes : (i + 1) * modes], state)
        partial[:, lanes] = state

    @pl.when(z == 0)
    def _():
        halo_in[...] = jnp.zeros_like(halo_in)

    @pl.when(z > 0)
    def _():
        send_halo.wait_recv()

    halo_rows[...] = halo_in[...].astype(F32)
    for j, buffer in enumerate((wide_q, wide_k, wide_v)):
        for c in range(rows):
            buffer[c, pl.ds(HEAD - 2, 2), :] = halo_rows[pl.ds(2 * j * pitch + c, 2, stride=pitch), :]
    for c in range(rows):
        lanes = slice(c * LANES, (c + 1) * LANES)
        value = filtered(1, wide_k, c, 0, HEAD) * filtered(2, wide_v, c, 0, HEAD)
        value = value.astype(BF16).astype(F32)
        gates[pl.ds(c, HEAD, stride=pitch), :] = value
        state = partial[:, lanes] + first_powers[0, :, lanes] * value[0:1] + first_powers[1, :, lanes] * value[1:2]
        half = c * 2 // rows
        state_out[pl.ds(half * modes, modes), slice((c - half * rows // 2) * LANES, (c - half * rows // 2 + 1) * LANES)] = state

    state_sent[...] = state_out[...].astype(BF16)
    state_copies = []
    for step in steps:
        copy = pltpu.make_async_remote_copy(
            src_ref=state_sent, dst_ref=state_in.at[step - 1],
            send_sem=state_send.at[step - 1], recv_sem=state_recv.at[step - 1],
            device_id={"seq": lax.rem(z + step, seq)}, device_id_type=MESH,
        )
        state_copies.append(copy)
    for step in steps:
        @pl.when(z + step < seq)
        def _():
            if step > 1:
                pl.semaphore_wait(ready.at[step - 1], 1)
            state_copies[step - 1].start()

        if 1 < step < reach_steps:
            tell(step + 1)

    def tile(ref, index):
        return ref[pl.ds(pl.multiple_of(index * pitch, pitch), pitch), :]

    decay = [jnp.exp(-tile(mode_rows, n)) for n in range(modes)]
    gain = [tile(mode_rows, modes + n) for n in range(modes)]
    load_q.wait()

    for step in steps:
        reach = (step - 1) * tokens
        open_ = jnp.float32(1.0)
        for first in starts:
            inside = (first >= offset - reach) & (first <= offset - 1)
            open_ = jnp.where(inside, 0.0, open_)

        @pl.when(z >= step)
        def _():
            state_copies[step - 1].wait_recv()
            came = state_in[step - 1].astype(F32)
            for c in range(rows):
                lanes = slice(c * LANES, (c + 1) * LANES)
                half = c * 2 // rows
                left = (c - half * rows // 2) * LANES
                part = came[half * modes : (half + 1) * modes, left : left + LANES] * open_
                if reach:
                    part = part * jnp.exp(wide_rates[:, lanes] * (-float(reach)))
                at = pl.ds(c, modes, stride=pitch)
                incoming[at, :] = incoming[at, :] + part

    own = g * sub + s
    carried = [tile(incoming, n) for n in range(modes)]
    unroll = 8

    def combine(parts):
        while len(parts) > 1:
            parts = [sum(parts[i + 1 : i + 2], parts[i]) for i in range(0, len(parts), 2)]
        return parts[0]

    def advance(block, state):
        for u in range(unroll):
            t = block * unroll + u
            gated, m1 = tile(gates, t), keep1[pl.ds(HEAD + t, 1), :]
            state = [decay[n] * (state[n] * m1) + gated for n in range(modes)]
            rows_out[pl.ds(pl.multiple_of(t * pitch, pitch), pitch), :] = combine(
                [gain[n] * state[n] for n in range(modes)]
            )
        return state

    def send(slot, c, axis, me, count, step, send_sem, recv_sem):
        lower, size, left, width = pieces[c]
        piece = gathered.at[1 + slot, pl.ds(lower, size), pl.ds(left, width)]
        return pltpu.make_async_remote_copy(
            src_ref=piece, dst_ref=piece, send_sem=send_sem, recv_sem=recv_sem,
            device_id={axis: lax.rem(me + step, count)}, device_id_type=MESH,
        )

    def over_sub(slot, c):
        return send(slot, c, "sub", s, sub, 1, sub_send.at[c], sub_recv.at[c])

    def over_grp(slot, c, step):
        return send(slot, c, "grp", g, grp, step, grp_send.at[step - 1, c], grp_recv.at[step - 1, c])

    def onward(slot, c, step):
        return send(slot, c, "sub", s, sub, 1, fwd_send.at[step - 1, c], fwd_recv.at[step - 1, c])

    for c, (lower, size, left, width) in enumerate(pieces):
        if c == 0:
            for block in range(size // unroll):
                carried = advance(block, carried)
        elif not left:
            carried = lax.fori_loop(lower // unroll, (lower + size) // unroll, advance, carried)

        def mix(r, carry):
            wide_q[r, pl.ds(HEAD + lower, size), :] = x_ref[0, pl.ds(lower, size), lanes_of(r)].astype(F32)
            long_out = rows_out[pl.ds(lower * pitch + r, size, stride=pitch), :]
            gathered[1 + own, pl.ds(lower, size), lanes_of(r)] = (
                filtered(0, wide_q, r, lower, size) * long_out
            ).astype(BF16)
            return carry

        if c == 0:
            for r in range(rows):
                mix(r, 0)
        else:
            lax.fori_loop(left // LANES, (left + width) // LANES, mix, 0)
        for step in range(1, grp):
            if c not in held:
                over_grp(own, c, step).start()
            else:
                pl.when(s == 0)(over_grp(own, c, step).start)
        over_sub(own, c).start()

    def product(slot, lower, count, left=0, width=channels):
        depth = pl.ds(pl.multiple_of(slot * channels + left, width), width)
        return jnp.dot(
            gathered[1 + slot, pl.ds(lower, count), pl.ds(left, width)], weight[depth, :],
            preferred_element_type=F32,
        )

    load_weight.wait()
    total[...] = product(own, 0, tokens)
    other = g * sub + 1 - s
    for c in range(len(pieces)):
        over_sub(other, c).wait_recv()
    total[...] += product(other, 0, tokens)

    def extent(members):
        return pieces[members[0]][0], sum(pieces[c][1] for c in members), *pieces[members[0]][2:]

    def direct(members):
        lower, count, left, width = extent(members)
        at = pl.ds(lower, count)
        for step in range(1, grp):
            slot = lax.rem(g + grp - step, grp) * sub + s
            for c in members:
                over_grp(slot, c, step).wait_recv()
                onward(slot, c, step).start()
            total[at, :] += product(slot, lower, count, left, width)

    def forwarded(members):
        lower, count, left, width = extent(members)
        at = pl.ds(lower, count)
        for step in range(1, grp):
            slot = lax.rem(g + grp - step, grp) * sub + 1 - s
            for c in members:
                onward(slot, c, step).wait_recv()
                if step == 1 and c == trigger:
                    @pl.when(s == 1)
                    def _():
                        for late in held:
                            for way in range(1, grp):
                                over_grp(own, late, way).start()
            value = total[at, :] + product(slot, lower, count, left, width)
            if step < grp - 1 or left + width < channels:
                total[at, :] = value
            else:
                out_ref[at, :] = value.astype(out_ref.dtype)

    for members in groupings[:-2]:
        direct(members)
        forwarded(members)
    for members in groupings[-2:]:
        direct(members)
    for members in groupings[-2:]:
        forwarded(members)

    for step in range(1, grp):
        for c in range(len(pieces)):
            over_grp(own, c, step).wait_send()
            onward(own, c, step).wait_send()
    for c in range(len(pieces)):
        over_sub(own, c).wait_send()
    pl.when(z < seq - 1)(send_halo.wait_send)
    for step in steps:
        pl.when(z + step < seq)(state_copies[step - 1].wait_send)


def shards(sizes, projected, short_filter, span_lengths, mode_rates, mode_residues, out_weight):
    seq, grp, sub = sizes
    tokens, _, channels = projected.shape
    modes, groups = mode_rates.shape
    rows = channels // LANES
    pitch = -(-rows // 8) * 8
    reach_steps = min(seq - 1, (seq * tokens // 2 - 1 + tokens - 1) // tokens)
    sizes_of = (16, 16, 32, 64, 64, 64)
    pieces = [(sum(sizes_of[:i]), size, 0, channels) for i, size in enumerate(sizes_of)]
    lower, size, left, width = pieces.pop()
    half = width // 2
    pieces = (*pieces, (lower, size, 0, half), (lower, size, half, half))
    count = len(pieces)
    groupings, trigger = ((0, 1, 2, 3), (4,), (5,), (6,)), 3
    per_row = LANES * groups // channels
    streams = projected.transpose(1, 0, 2)
    vmem = pl.BlockSpec(memory_space=pltpu.VMEM)
    hbm = pl.BlockSpec(memory_space=pl.ANY)
    dma = pltpu.SemaphoreType.DMA
    row_tile = pltpu.VMEM((tokens * pitch, LANES), F32)
    stream = pltpu.VMEM((rows, tokens + HEAD, LANES), F32)
    state, packed = (modes, channels), (2 * modes, channels // 2)
    return pl.pallas_call(
        functools.partial(kernel, (seq, grp, sub, reach_steps, pieces, groupings, trigger)),
        out_shape=pltpu.VMEM((tokens, out_weight.shape[1]), BF16),
        in_specs=[hbm] * 6,
        out_specs=vmem,
        scratch_shapes=[
            pltpu.SMEM(span_lengths.shape, jnp.int32),
            pltpu.VMEM(streams.shape, BF16),
            pltpu.VMEM((3, EDGE, channels), BF16),
            pltpu.VMEM(short_filter.shape, F32),
            pltpu.VMEM(mode_rates.shape, F32),
            pltpu.VMEM(mode_residues.shape, F32),
            pltpu.VMEM(out_weight.shape, BF16),
            stream, stream, stream,
            pltpu.VMEM((tokens + HEAD, LANES), F32),
            pltpu.VMEM((tokens, LANES), F32),
            pltpu.VMEM((rows, 2 * per_row * modes, tokens), F32),
            pltpu.VMEM((2 * modes * pitch, LANES), F32),
            pltpu.VMEM(state, F32),
            pltpu.VMEM((2,) + state, F32),
            pltpu.VMEM(state, F32),
            row_tile, row_tile,
            pltpu.VMEM((6 * pitch, LANES), F32),
            pltpu.VMEM((6 * pitch, LANES), BF16),
            pltpu.VMEM((6 * pitch, LANES), BF16),
            pltpu.VMEM(packed, F32),
            pltpu.VMEM(packed, BF16),
            pltpu.VMEM((reach_steps,) + packed, BF16),
            pltpu.VMEM((modes * pitch, LANES), F32),
            pltpu.VMEM((1 + grp * sub, tokens, channels), BF16),
            pltpu.VMEM((tokens, out_weight.shape[1]), F32),
            dma((7,)), dma, pltpu.SemaphoreType.REGULAR((reach_steps,)), dma, dma,
            dma((reach_steps,)), dma((reach_steps,)),
            dma((count,)), dma((count,)),
            dma((grp - 1, count)), dma((grp - 1, count)),
            dma((grp - 1, count)), dma((grp - 1, count)),
        ],
        compiler_params=pltpu.CompilerParams(collective_id=0, has_side_effects=True),
    )(span_lengths, streams, short_filter, mode_rates, mode_residues, out_weight)


def solution(mesh):
    sizes = (mesh.shape["seq"], mesh.shape["grp"], mesh.shape["sub"])
    return jax.shard_map(
        functools.partial(shards, sizes),
        mesh=mesh,
        in_specs=(
            P(("parts", "seq"), None, ("grp", "sub")),
            P(None, None, ("grp", "sub")),
            P("parts"),
            P(None, ("grp", "sub")),
            P(None, ("grp", "sub")),
            P(None, ("grp", "sub")),
        ),
        out_specs=P(("parts", "seq"), ("grp", "sub")),
        check_vma=False,
    )
```

```python
import functools

import jax
import jax.numpy as jnp
from jax import lax
from jax.experimental import pallas as pl
from jax.experimental.pallas import tpu as pltpu
from jax.sharding import PartitionSpec as P

MESH = pl.DeviceIdType.MESH
LANES = 128
HEAD = 8
EDGE = 16
F32, BF16 = jnp.float32, jnp.bfloat16


def tanh(x):
    x = jnp.clip(x, -7.90531110763549805, 7.90531110763549805)
    square = x * x
    top = jnp.full_like(x, -2.76076847742355e-16)
    for c in (
        2.00018790482477e-13, -8.60467152213735e-11, 5.12229709037114e-08,
        1.48572235717979e-05, 6.37261928875436e-04, 4.89352455891786e-03,
    ):
        top = top * square + c
    bottom = jnp.full_like(x, 1.19825839466702e-06)
    for c in (1.18534705686654e-04, 2.26843463243900e-03, 4.89352518554385e-03):
        bottom = bottom * square + c
    return jnp.where(jnp.abs(x) < 0.0004, x, x * top / bottom)


def kernel(
    sizes, spans_hbm, x_hbm, taps_hbm, rates_hbm, residues_hbm, weight_hbm, out_ref,
    spans_ref, x_ref, edge_ref, taps_ref, rates_ref, residues_ref, weight,
    wide_q, wide_k, wide_v, keep1, keep2, powers, mode_rows, wide_rates, first_powers, partial,
    gates, rows_out, halo_rows, halo_out, halo_in, state_out, state_sent, state_in, incoming,
    gathered, total,
    load_sems, weight_sem, ready, halo_send, halo_recv, state_send, state_recv,
    sub_send, sub_recv, grp_send, grp_recv, fwd_send, fwd_recv,
):
    seq, grp, sub, reach_steps, pieces, groupings, trigger = sizes
    _, tokens, channels = x_ref.shape
    modes, groups = rates_ref.shape
    held = range(len(pieces) - 2, len(pieces))
    rows = channels // LANES
    pitch = gates.shape[0] // tokens
    group_size = channels // groups
    per_row = LANES // group_size
    steps = range(1, reach_steps + 1)
    z, g, s = lax.axis_index("seq"), lax.axis_index("grp"), lax.axis_index("sub")
    offset = z * tokens

    barrier = pltpu.get_barrier_semaphore()
    @pl.when(z > 0)
    def _():
        pl.semaphore_signal(barrier, inc=1, device_id={"seq": z - 1}, device_id_type=MESH)

    @pl.when(z < seq - 1)
    def _():
        pl.semaphore_signal(barrier, inc=1, device_id={"seq": z + 1}, device_id_type=MESH)

    for axis, me, count in (("grp", g, grp), ("sub", s, sub)):
        for step in range(1, count):
            pl.semaphore_signal(
                barrier, inc=1, device_id={axis: lax.rem(me + step, count)}, device_id_type=MESH
            )
    loads = [
        pltpu.make_async_copy(source, target, load_sems.at[i])
        for i, (source, target) in enumerate((
            (rates_hbm, rates_ref), (residues_hbm, residues_ref), (spans_hbm, spans_ref),
            (x_hbm.at[:, pl.ds(tokens - EDGE, EDGE), :], edge_ref), (taps_hbm, taps_ref),
            (x_hbm.at[pl.ds(1, 2)], x_ref.at[pl.ds(1, 2)]), (x_hbm.at[pl.ds(0, 1)], x_ref.at[pl.ds(0, 1)]),
        ))
    ]
    load_rates, load_residues, load_spans, load_edge, load_taps, load_kv, load_q = loads
    for load in loads:
        load.start()

    load_weight = pltpu.make_async_copy(weight_hbm, weight, weight_sem)
    load_weight.start()

    if pitch != rows:
        for buffer in (gates, mode_rows):
            buffer[...] = jnp.zeros_like(buffer)
    incoming[...] = jnp.zeros_like(incoming)
    for buffer in (wide_k, wide_v):
        buffer[:, pl.ds(0, HEAD), :] = jnp.zeros((rows, HEAD, LANES), F32)

    load_spans.wait()
    starts, start = [], jnp.int32(0)
    for i in range(spans_ref.shape[0]):
        starts.append(start)
        start = start + spans_ref[i]
    latest = jnp.int32(0)
    for first in starts:
        latest = jnp.where(first < offset + tokens, first, latest)
    position = offset - HEAD + lax.broadcasted_iota(jnp.int32, (tokens + HEAD, LANES), 0)
    here = position == starts[0]
    for first in starts[1:]:
        here = here | (position == first)
    keep1[...] = jnp.where(here, 0.0, 1.0)
    keep2[...] = keep1[pl.ds(HEAD, tokens), :] * keep1[pl.ds(HEAD - 1, tokens), :]

    load_rates.wait()
    load_residues.wait()
    rates = rates_ref[...]
    token = lax.broadcasted_iota(jnp.int32, (modes, tokens), 1)
    ahead = (token - (tokens - 1)).astype(F32)
    live = jnp.where((offset + token >= latest) & (token >= 2), 1.0, 0.0)
    for c in range(rows):
        for i in range(0, per_row, 2):
            pair = []
            for j in (i, i + 1):
                at = c * per_row + j
                pair.append(jnp.exp(jnp.broadcast_to(rates[:, at : at + 1], (modes, tokens)) * ahead) * live)
            power = jnp.concatenate(pair, axis=0)
            high = power.astype(BF16)
            powers[c, pl.ds(i * modes, 2 * modes), :] = high
            low = power - high.astype(F32)
            powers[c, pl.ds((per_row + i) * modes, 2 * modes), :] = low.astype(BF16)

    spread = (
        lax.broadcasted_iota(jnp.int32, (groups, channels), 1) // group_size
        == lax.broadcasted_iota(jnp.int32, (groups, channels), 0)
    ).astype(F32)
    drop = tanh(rates) * (1.0 + jnp.exp(-2.0 * rates))
    for first, values in ((0, rates), (modes, residues_ref[...] * jnp.sqrt(drop))):
        wide = jnp.dot(values, spread, precision=lax.Precision.HIGHEST, preferred_element_type=F32)
        if first == 0:
            wide_rates[...] = wide
            for t in range(2):
                first_live = jnp.where(offset + t >= latest, 1.0, 0.0)
                first_powers[t] = jnp.exp(wide * (-float(tokens - 1 - t))) * first_live
        for c in range(rows):
            mode_rows[pl.ds(first * pitch + c, modes, stride=pitch), :] = wide[
                :, c * LANES : (c + 1) * LANES
            ]

    load_edge.wait()
    for j in range(3):
        for c in range(rows):
            lanes = slice(c * LANES, (c + 1) * LANES)
            halo_rows[pl.ds(2 * j * pitch + c, 2, stride=pitch), :] = edge_ref[j, :, lanes].astype(F32)[EDGE - 2 :]
    halo_out[...] = halo_rows[...].astype(BF16)

    pl.semaphore_wait(barrier, jnp.minimum(seq - 1 - z, 1) + jnp.minimum(z, 1) + grp + sub - 2)

    send_halo = pltpu.make_async_remote_copy(
        src_ref=halo_out, dst_ref=halo_in, send_sem=halo_send, recv_sem=halo_recv,
        device_id={"seq": lax.rem(z + 1, seq)}, device_id_type=MESH,
    )

    @pl.when(z < seq - 1)
    def _():
        send_halo.start()

    def tell(step):
        @pl.when((z > 0) & (z + step - 1 < seq))
        def _():
            pl.semaphore_signal(
                ready.at[step - 1], inc=1, device_id={"seq": z - 1}, device_id_type=MESH
            )

    if reach_steps > 1:
        tell(2)

    load_taps.wait()

    def lanes_of(c):
        if isinstance(c, int):
            return slice(c * LANES, (c + 1) * LANES)
        return pl.ds(pl.multiple_of(c * LANES, LANES), LANES)

    def filtered(j, buffer, c, lower, count):
        tap = [taps_ref[k, pl.ds(j, 1), lanes_of(c)] for k in range(3)]
        now, last, older = (buffer[c, pl.ds(HEAD + lower - k, count), :] for k in range(3))
        m1, m2 = keep1[pl.ds(HEAD + lower, count), :], keep2[pl.ds(lower, count), :]
        return tap[0] * now + tap[1] * last * m1 + tap[2] * older * m2

    def gate(c, lower, count):
        value = (filtered(1, wide_k, c, lower, count) * filtered(2, wide_v, c, lower, count)).astype(BF16)
        gathered[0, pl.ds(lower, count), lanes_of(c)] = value
        gates[pl.ds(lower * pitch + c, count, stride=pitch), :] = value.astype(F32)

    load_kv.wait()
    block = 64

    def gate_rows(c, carry):
        for j, buffer in ((1, wide_k), (2, wide_v)):
            buffer[c, pl.ds(HEAD, tokens), :] = x_ref[j, :, lanes_of(c)].astype(F32)
        lower = 0
        while lower < tokens:
            count = min(block, tokens - lower)
            gate(c, lower, count)
            lower += count
        return carry

    lax.fori_loop(0, rows, gate_rows, 0)

    lane_group = lax.broadcasted_iota(jnp.int32, (modes, LANES), 1) // group_size
    for c in range(rows):
        lanes = slice(c * LANES, (c + 1) * LANES)
        sums = jnp.dot(powers[c], gathered[0, :, lanes], preferred_element_type=F32)
        sums = sums[: per_row * modes] + sums[per_row * modes :]
        state = sums[:modes]
        for i in range(1, per_row):
            state = jnp.where(lane_group == i, sums[i * modes : (i + 1) * modes], state)
        partial[:, lanes] = state

    @pl.when(z == 0)
    def _():
        halo_in[...] = jnp.zeros_like(halo_in)

    @pl.when(z > 0)
    def _():
        send_halo.wait_recv()

    halo_rows[...] = halo_in[...].astype(F32)
    for j, buffer in enumerate((wide_q, wide_k, wide_v)):
        for c in range(rows):
            buffer[c, pl.ds(HEAD - 2, 2), :] = halo_rows[pl.ds(2 * j * pitch + c, 2, stride=pitch), :]
    for c in range(rows):
        lanes = slice(c * LANES, (c + 1) * LANES)
        value = filtered(1, wide_k, c, 0, HEAD) * filtered(2, wide_v, c, 0, HEAD)
        value = value.astype(BF16).astype(F32)
        gates[pl.ds(c, HEAD, stride=pitch), :] = value
        state = partial[:, lanes] + first_powers[0, :, lanes] * value[0:1] + first_powers[1, :, lanes] * value[1:2]
        half = c * 2 // rows
        state_out[pl.ds(half * modes, modes), slice((c - half * rows // 2) * LANES, (c - half * rows // 2 + 1) * LANES)] = state

    state_sent[...] = state_out[...].astype(BF16)
    state_copies = []
    for step in steps:
        copy = pltpu.make_async_remote_copy(
            src_ref=state_sent, dst_ref=state_in.at[step - 1],
            send_sem=state_send.at[step - 1], recv_sem=state_recv.at[step - 1],
            device_id={"seq": lax.rem(z + step, seq)}, device_id_type=MESH,
        )
        state_copies.append(copy)
    for step in steps:
        @pl.when(z + step < seq)
        def _():
            if step > 1:
                pl.semaphore_wait(ready.at[step - 1], 1)
            state_copies[step - 1].start()

        if 1 < step < reach_steps:
            tell(step + 1)

    def tile(ref, index):
        return ref[pl.ds(pl.multiple_of(index * pitch, pitch), pitch), :]

    decay = [jnp.exp(-tile(mode_rows, n)) for n in range(modes)]
    gain = [tile(mode_rows, modes + n) for n in range(modes)]
    load_q.wait()

    for step in steps:
        reach = (step - 1) * tokens
        open_ = jnp.float32(1.0)
        for first in starts:
            inside = (first >= offset - reach) & (first <= offset - 1)
            open_ = jnp.where(inside, 0.0, open_)

        @pl.when(z >= step)
        def _():
            state_copies[step - 1].wait_recv()
            came = state_in[step - 1].astype(F32)
            for c in range(rows):
                lanes = slice(c * LANES, (c + 1) * LANES)
                half = c * 2 // rows
                left = (c - half * rows // 2) * LANES
                part = came[half * modes : (half + 1) * modes, left : left + LANES] * open_
                if reach:
                    part = part * jnp.exp(wide_rates[:, lanes] * (-float(reach)))
                at = pl.ds(c, modes, stride=pitch)
                incoming[at, :] = incoming[at, :] + part

    own = g * sub + s
    carried = [tile(incoming, n) for n in range(modes)]
    unroll = 8

    def combine(parts):
        while len(parts) > 1:
            parts = [sum(parts[i + 1 : i + 2], parts[i]) for i in range(0, len(parts), 2)]
        return parts[0]

    def advance(block, state):
        for u in range(unroll):
            t = block * unroll + u
            gated, m1 = tile(gates, t), keep1[pl.ds(HEAD + t, 1), :]
            state = [decay[n] * (state[n] * m1) + gated for n in range(modes)]
            rows_out[pl.ds(pl.multiple_of(t * pitch, pitch), pitch), :] = combine(
                [gain[n] * state[n] for n in range(modes)]
            )
        return state

    def send(slot, c, axis, me, count, step, send_sem, recv_sem):
        lower, size, left, width = pieces[c]
        piece = gathered.at[1 + slot, pl.ds(lower, size), pl.ds(left, width)]
        return pltpu.make_async_remote_copy(
            src_ref=piece, dst_ref=piece, send_sem=send_sem, recv_sem=recv_sem,
            device_id={axis: lax.rem(me + step, count)}, device_id_type=MESH,
        )

    def over_sub(slot, c):
        return send(slot, c, "sub", s, sub, 1, sub_send.at[c], sub_recv.at[c])

    def over_grp(slot, c, step):
        return send(slot, c, "grp", g, grp, step, grp_send.at[step - 1, c], grp_recv.at[step - 1, c])

    def onward(slot, c, step):
        return send(slot, c, "sub", s, sub, 1, fwd_send.at[step - 1, c], fwd_recv.at[step - 1, c])

    for c, (lower, size, left, width) in enumerate(pieces):
        carried = carried if left else lax.fori_loop(lower // unroll, (lower + size) // unroll, advance, carried)

        def mix(r, carry):
            wide_q[r, pl.ds(HEAD + lower, size), :] = x_ref[0, pl.ds(lower, size), lanes_of(r)].astype(F32)
            long_out = rows_out[pl.ds(lower * pitch + r, size, stride=pitch), :]
            gathered[1 + own, pl.ds(lower, size), lanes_of(r)] = (
                filtered(0, wide_q, r, lower, size) * long_out
            ).astype(BF16)
            return carry

        if c == 0:
            for r in range(rows):
                mix(r, 0)
        else:
            lax.fori_loop(left // LANES, (left + width) // LANES, mix, 0)
        for step in range(1, grp):
            if c not in held:
                over_grp(own, c, step).start()
            else:
                pl.when(s == 0)(over_grp(own, c, step).start)
        over_sub(own, c).start()

    def product(slot, lower, count, left=0, width=channels):
        depth = pl.ds(pl.multiple_of(slot * channels + left, width), width)
        return jnp.dot(
            gathered[1 + slot, pl.ds(lower, count), pl.ds(left, width)], weight[depth, :],
            preferred_element_type=F32,
        )

    load_weight.wait()
    total[...] = product(own, 0, tokens)
    other = g * sub + 1 - s
    for c in range(len(pieces)):
        over_sub(other, c).wait_recv()
    total[...] += product(other, 0, tokens)

    def extent(members):
        return pieces[members[0]][0], sum(pieces[c][1] for c in members), *pieces[members[0]][2:]

    def direct(members):
        lower, count, left, width = extent(members)
        at = pl.ds(lower, count)
        for step in range(1, grp):
            slot = lax.rem(g + grp - step, grp) * sub + s
            for c in members:
                over_grp(slot, c, step).wait_recv()
                onward(slot, c, step).start()
            total[at, :] += product(slot, lower, count, left, width)

    def forwarded(members):
        lower, count, left, width = extent(members)
        at = pl.ds(lower, count)
        for step in range(1, grp):
            slot = lax.rem(g + grp - step, grp) * sub + 1 - s
            for c in members:
                onward(slot, c, step).wait_recv()
                if step == 1 and c == trigger:
                    @pl.when(s == 1)
                    def _():
                        for late in held:
                            for way in range(1, grp):
                                over_grp(own, late, way).start()
            value = total[at, :] + product(slot, lower, count, left, width)
            if step < grp - 1 or left + width < channels:
                total[at, :] = value
            else:
                out_ref[at, :] = value.astype(out_ref.dtype)

    for members in groupings[:-2]:
        direct(members)
        forwarded(members)
    for members in groupings[-2:]:
        direct(members)
    for members in groupings[-2:]:
        forwarded(members)

    for step in range(1, grp):
        for c in range(len(pieces)):
            over_grp(own, c, step).wait_send()
            onward(own, c, step).wait_send()
    for c in range(len(pieces)):
        over_sub(own, c).wait_send()
    pl.when(z < seq - 1)(send_halo.wait_send)
    for step in steps:
        pl.when(z + step < seq)(state_copies[step - 1].wait_send)


def shards(sizes, projected, short_filter, span_lengths, mode_rates, mode_residues, out_weight):
    seq, grp, sub = sizes
    tokens, _, channels = projected.shape
    modes, groups = mode_rates.shape
    rows = channels // LANES
    pitch = -(-rows // 8) * 8
    reach_steps = min(seq - 1, (seq * tokens // 2 - 1 + tokens - 1) // tokens)
    sizes_of = (16, 16, 32, 64, 64, 64)
    pieces = [(sum(sizes_of[:i]), size, 0, channels) for i, size in enumerate(sizes_of)]
    lower, size, left, width = pieces.pop()
    half = width // 2
    pieces = (*pieces, (lower, size, 0, half), (lower, size, half, half))
    count = len(pieces)
    groupings, trigger = ((0, 1, 2, 3), (4,), (5,), (6,)), 3
    per_row = LANES * groups // channels
    streams = projected.transpose(1, 0, 2)
    vmem = pl.BlockSpec(memory_space=pltpu.VMEM)
    hbm = pl.BlockSpec(memory_space=pl.ANY)
    dma = pltpu.SemaphoreType.DMA
    row_tile = pltpu.VMEM((tokens * pitch, LANES), F32)
    stream = pltpu.VMEM((rows, tokens + HEAD, LANES), F32)
    state, packed = (modes, channels), (2 * modes, channels // 2)
    return pl.pallas_call(
        functools.partial(kernel, (seq, grp, sub, reach_steps, pieces, groupings, trigger)),
        out_shape=pltpu.VMEM((tokens, out_weight.shape[1]), BF16),
        in_specs=[hbm] * 6,
        out_specs=vmem,
        scratch_shapes=[
            pltpu.SMEM(span_lengths.shape, jnp.int32),
            pltpu.VMEM(streams.shape, BF16),
            pltpu.VMEM((3, EDGE, channels), BF16),
            pltpu.VMEM(short_filter.shape, F32),
            pltpu.VMEM(mode_rates.shape, F32),
            pltpu.VMEM(mode_residues.shape, F32),
            pltpu.VMEM(out_weight.shape, BF16),
            stream, stream, stream,
            pltpu.VMEM((tokens + HEAD, LANES), F32),
            pltpu.VMEM((tokens, LANES), F32),
            pltpu.VMEM((rows, 2 * per_row * modes, tokens), BF16),
            pltpu.VMEM((2 * modes * pitch, LANES), F32),
            pltpu.VMEM(state, F32),
            pltpu.VMEM((2,) + state, F32),
            pltpu.VMEM(state, F32),
            row_tile, row_tile,
            pltpu.VMEM((6 * pitch, LANES), F32),
            pltpu.VMEM((6 * pitch, LANES), BF16),
            pltpu.VMEM((6 * pitch, LANES), BF16),
            pltpu.VMEM(packed, F32),
            pltpu.VMEM(packed, BF16),
            pltpu.VMEM((reach_steps,) + packed, BF16),
            pltpu.VMEM((modes * pitch, LANES), F32),
            pltpu.VMEM((1 + grp * sub, tokens, channels), BF16),
            pltpu.VMEM((tokens, out_weight.shape[1]), F32),
            dma((7,)), dma, pltpu.SemaphoreType.REGULAR((reach_steps,)), dma, dma,
            dma((reach_steps,)), dma((reach_steps,)),
            dma((count,)), dma((count,)),
            dma((grp - 1, count)), dma((grp - 1, count)),
            dma((grp - 1, count)), dma((grp - 1, count)),
        ],
        compiler_params=pltpu.CompilerParams(collective_id=0, has_side_effects=True),
    )(span_lengths, streams, short_filter, mode_rates, mode_residues, out_weight)


def solution(mesh):
    sizes = (mesh.shape["seq"], mesh.shape["grp"], mesh.shape["sub"])
    return jax.shard_map(
        functools.partial(shards, sizes),
        mesh=mesh,
        in_specs=(
            P(("parts", "seq"), None, ("grp", "sub")),
            P(None, None, ("grp", "sub")),
            P("parts"),
            P(None, ("grp", "sub")),
            P(None, ("grp", "sub")),
            P(None, ("grp", "sub")),
        ),
        out_specs=P(("parts", "seq"), ("grp", "sub")),
        check_vma=False,
    )
```
